512 devices in a mesh: wide: 64 (over x, y, z_hi, core), narrow: 8 (over z_lo).
Axes of the slice: x: 4, y: 4, z: 16 (z_hi: 2, z_lo: 8; z = z_hi * 8 + z_lo), core: 2. Of those that a mesh axis runs over, the one named last changes fastest.
Arguments:
- electric: float32 [3, 3, 512, 192, 128], P(None, None, 'wide', 'narrow'), may hold values from -6 to 6
- magnetic: float32 [3, 3, 512, 192, 128], P(None, None, 'wide', 'narrow'), may hold values from -6 to 6
- current: float32 [3, 512, 192, 128], P(None, 'wide', 'narrow'), may hold values from -6 to 6
- density_tiles: float32 [256, 96, 64], P('wide', 'narrow'), may hold values from 0 to 1
- tile_slabs: int32 [64], replicated, may hold values from 0 to 63, each once
- design_box: int32 [6], replicated, may hold values from 0 to 512, as said below
- material_mask: int32 [512, 192, 128], P('wide', 'narrow'), may hold values 0 or 1
- material_levels: float32 [2], replicated, may hold values from 2 to 12
Outputs:
- final_electric: float32 [3, 3, 512, 192, 128], P(None, None, 'wide', 'narrow')
- final_magnetic: float32 [3, 3, 512, 192, 128], P(None, None, 'wide', 'narrow')
The draws below stay inside these ranges and needn't reach their ends.
Inputs may be any that keep to these rules, and one draw needn't show every extreme that they name: `tile_slabs`: each slab index appears exactly once. `design_box`: along each dimension of n cells the low bound is below n // 4; the high bound is 512 along the first dimension, at least 168 along the second, and at least n // 2 along the third.
All inputs are finite; a program needn't handle non-finite values. No bound on the sum of `material_mask` on one device may be relied on, other than what follows from the above.
Results may differ from the reference program's by a relative error of at most 0.00013.
Values sent between devices are 32-bit elements; how exact they have to be, the bound alone decides.
No kernel may reach another device: no remote copies, remote signals or barrier semaphores. Data moves between devices by JAX's collectives and lax.ppermute only.
A program may use at most 64 MiB of HBM per device.

```python
import jax
import jax.numpy as jnp
from jax import lax

CX = 8
CY = 24
STEPS = 4
REALS = 3
NX = 512
NY = 192
NZ = 128
N_WIDE = 64


def draw_design_box(key, part):
    subkeys = jax.random.split(key, 6)
    x_low = jax.random.randint(subkeys[0], (1,), 0, NX // 4, dtype=jnp.int32)
    x_high = jnp.full((1,), NX, dtype=jnp.int32)
    y_low = jax.random.randint(subkeys[2], (1,), 0, NY // 4, dtype=jnp.int32)
    y_high = jax.random.randint(subkeys[3], (1,), NY - CY, NY + 1, dtype=jnp.int32)
    z_low = jax.random.randint(subkeys[4], (1,), 0, NZ // 4, dtype=jnp.int32)
    z_high = jax.random.randint(subkeys[5], (1,), NZ // 2, NZ + 1, dtype=jnp.int32)
    return jnp.concatenate([x_low, x_high, y_low, y_high, z_low, z_high]).astype(jnp.int32)


def place_ends(entries, stream_key, low, top_value):
    place = [jax.random.randint(jax.random.fold_in(stream_key, axis), (), 0, length) for axis, length in enumerate(entries.shape)]
    longest = entries.shape.index(max(entries.shape))
    next_to = place[:longest] + [(place[longest] + 1) % entries.shape[longest]] + place[longest + 1:]
    return entries.at[tuple(place)].set(low).at[tuple(next_to)].set(top_value)


def block_levels(rng, dims, cuts, smallest, top_value):
    def one(position, shards_of):
        heights = jax.random.uniform(jax.random.fold_in(jax.random.fold_in(rng, 6), position), (shards_of,), jnp.float32, smallest / len(cuts), top_value / len(cuts))
        return jnp.repeat(jnp.exp(heights), dims[position] // shards_of).reshape((-1,) + (1,) * (len(dims) - position - 1))

    factor_of = one(*cuts[0])
    for cut in cuts[1:]:
        factor_of = factor_of * one(*cut)
    return factor_of


def normal_values(key, dims, spread, most, cuts=(), kind=jnp.bfloat16):
    factor_of = block_levels(key, dims, cuts, -0.22, 0.18) if cuts else 1.0
    drawn = jax.random.normal(key, dims, jnp.float32) * spread * factor_of
    return jnp.minimum(jnp.maximum(drawn, -most), most).astype(kind)


def setup_inputs(seed: int = 0) -> dict:
    seeds = jax.random.split(jax.random.key(seed), 9)
    electric = normal_values(seeds[0], (REALS, 3, NX, NY, NZ), 1.0, 6.0, ((2, 64), (3, 8)), jnp.float32)
    magnetic = normal_values(seeds[1], (REALS, 3, NX, NY, NZ), 1.0, 6.0, ((2, 64), (3, 8)), jnp.float32)
    current = normal_values(seeds[2], (3, NX, NY, NZ), 1.0, 6.0, ((1, 64), (2, 8)), jnp.float32)
    density_tiles = jnp.clip(1.0 * jax.random.uniform(seeds[3], (NX // 2, NY // 2, NZ // 2), jnp.float32) ** block_levels(seeds[3], (NX // 2, NY // 2, NZ // 2), ((0, 64), (1, 8)), -0.2, 0.2), 0.0, 1.0)
    tile_slabs = jax.random.permutation(seeds[4], N_WIDE).astype(jnp.int32)
    design_box = draw_design_box(jax.random.fold_in(seeds[8], 71), 0)
    material_mask = place_ends((jax.random.randint(seeds[6], (NX, NY, NZ), 0, 2) < 1).astype(jnp.int32), jax.random.fold_in(seeds[6], 1), 0, 1)
    material_levels = jnp.clip(jax.random.uniform(seeds[7], (2,), jnp.float32, 2.0, 12.0), 2.0, 12.0)
    return dict(electric=electric, magnetic=magnetic, current=current, density_tiles=density_tiles, tile_slabs=tile_slabs, design_box=design_box, material_mask=material_mask, material_levels=material_levels)


sharpness = 8.0
thresholds = (0.7, 0.5, 0.3)
time_step = 0.5


def project(filtered, threshold):
    numer = jnp.tanh(sharpness * threshold) + jnp.tanh(sharpness * (filtered - threshold))
    denom = jnp.tanh(sharpness * threshold) + jnp.tanh(sharpness * (1.0 - threshold))
    return numer / denom


def refine(extended, dimension):
    cells_in = extended.shape[dimension] - 1
    lower_cells = lax.slice_in_dim(extended, 0, cells_in, axis=dimension)
    higher_cells = lax.slice_in_dim(extended, 1, cells_in + 1, axis=dimension)
    middle = 0.5 * (lower_cells + higher_cells)
    paired = jnp.stack([lower_cells, middle], axis=dimension + 1)
    new_shape = list(extended.shape)
    new_shape[dimension] = 2 * cells_in
    return paired.reshape(new_shape)


def forward(component, upper_face, dimension):
    length = component.shape[dimension]
    shifted_up = jnp.concatenate([lax.slice_in_dim(component, 1, length, axis=dimension), upper_face], axis=dimension)
    return shifted_up - component


def backward(component, lower_face, dimension):
    length = component.shape[dimension]
    behind = jnp.concatenate([lower_face, lax.slice_in_dim(component, 0, length - 1, axis=dimension)], axis=dimension)
    return component - behind


def curl(components, faces, difference):
    def slope(member, dimension):
        return difference(components[member], faces[(dimension, member)], dimension + 1)
    return [slope(2, 1) - slope(1, 2), slope(0, 2) - slope(2, 0), slope(1, 0) - slope(0, 1)]


def zero_faces(sample):
    faces = {}
    for dimension in range(3):
        face_shape = list(sample.shape)
        face_shape[dimension + 1] = 1
        for member in range(3):
            faces[(dimension, member)] = jnp.zeros(face_shape, sample.dtype)
    return faces


def reference(electric, magnetic, current, density_tiles, tile_slabs, design_box, material_mask, material_levels):
    tile_blocks = density_tiles.reshape(N_WIDE, CX // 2, NY // 2, NZ // 2)
    inverse = jnp.zeros((N_WIDE,), jnp.int32).at[tile_slabs].set(jnp.arange(N_WIDE, dtype=jnp.int32))
    coarse = jnp.take(tile_blocks, inverse, axis=0).reshape(NX // 2, NY // 2, NZ // 2)
    for dimension in range(3):
        length = coarse.shape[dimension]
        edge = lax.slice_in_dim(coarse, length - 1, length, axis=dimension)
        coarse = refine(jnp.concatenate([coarse, edge], axis=dimension), dimension)
    projected = jnp.stack([project(coarse, threshold) for threshold in thresholds])
    global_x = jnp.arange(NX, dtype=jnp.int32)
    global_y = jnp.arange(NY, dtype=jnp.int32)
    global_z = jnp.arange(NZ, dtype=jnp.int32)
    inside = (((global_x >= design_box[0]) & (global_x < design_box[1]))[:, None, None]
              & ((global_y >= design_box[2]) & (global_y < design_box[3]))[None, :, None]
              & ((global_z >= design_box[4]) & (global_z < design_box[5]))[None, None, :])
    background = jnp.where(material_mask == 1, material_levels[1], material_levels[0])
    design = material_levels[0] + projected * (material_levels[1] - material_levels[0])
    permittivity = jnp.where(inside[None], design, background[None])
    coefficient = time_step / permittivity
    faces = zero_faces(electric[:, 0])
    for iteration in range(STEPS):
        curl_e = curl([electric[:, member] for member in range(3)], faces, forward)
        magnetic = jnp.stack([magnetic[:, member] - time_step * curl_e[member] for member in range(3)], axis=1)
        curl_h = curl([magnetic[:, member] for member in range(3)], faces, backward)
        electric = jnp.stack([electric[:, member] + coefficient * (curl_h[member] - current[member]) for member in range(3)], axis=1)
    return electric, magnetic
```

```python
import jax
import jax.numpy as jnp
import numpy as np
from jax import lax
from jax.experimental import pallas as pl
from jax.experimental.pallas import tpu as pltpu
from jax.sharding import PartitionSpec as P

STEPS = 4
PLANES = 8
OWN = 24
ROWS = 32
HALO = 4
LANES = 128
TILES = 28

sharpness = 8.0
thresholds = (0.7, 0.5, 0.3)
time_step = 0.5

INTERPRET = False


def lane_ids():
    return lax.broadcasted_iota(jnp.int32, (ROWS, LANES), 1)


def row_ids():
    rows = lax.broadcasted_iota(jnp.int32, (ROWS, LANES), 0)
    return jnp.where(rows < OWN + HALO, rows, rows - ROWS)


def y_forward(a):
    return pltpu.roll(a, ROWS - 1, 0) - a


def y_backward(a):
    return a - pltpu.roll(a, 1, 0)


def z_forward(a, lanes):
    return jnp.where(lanes == LANES - 1, 0.0, pltpu.roll(a, LANES - 1, 1)) - a


def z_backward(a, lanes):
    return a - jnp.where(lanes == 0, 0.0, pltpu.roll(a, 1, 1))


def next_magnetic(h, e, e_up, step, lanes):
    up_y, up_z = e_up
    curl_x = y_forward(e[2]) - z_forward(e[1], lanes)
    curl_y = z_forward(e[0], lanes) - (up_z - e[2])
    curl_z = (up_y - e[1]) - y_forward(e[0])
    return [h[0] - step * curl_x, h[1] - step * curl_y, h[2] - step * curl_z]


def next_electric(e, h, h_down, coefficient, current, lanes):
    down_y, down_z = h_down
    curls = [
        y_backward(h[2]) - z_backward(h[1], lanes),
        z_backward(h[0], lanes) - (h[2] - down_z),
        (h[1] - down_y) - y_backward(h[0]),
    ]
    if current is not None:
        curls = [curls[c] - current[c] for c in range(3)]
    return [e[c] + coefficient * curls[c] for c in range(3)]


def step_of_rows(narrow_place):
    return jnp.where((row_ids() < 0) & (narrow_place == 0), 0.0, time_step)


WIDE, NARROW, CORE, WIDE_COUNT, NARROW_COUNT, OWN_AT, BEFORE_AT, AFTER_AT, BOX = 0, 1, 2, 3, 4, 5, 6, 7, 8


def extend_kernel(table, e_ref, h_ref, j_ref, m_ref, lo_ref, hi_ref, ee_ref, h1_ref, jj_ref, mm_ref):
    lanes = lane_ids()
    step = step_of_rows(table[NARROW])

    def extended(own, at):
        return jnp.concatenate([own, hi_ref[at], lo_ref[at]], axis=0)

    def per_real(r, carry):
        def fields(p):
            return [extended(e_ref[r, c, p], (r * 3 + c) * PLANES + p) for c in range(3)]

        up = fields(PLANES - 1)
        for p in range(PLANES - 1, -1, -1):
            e = up if p == PLANES - 1 else fields(p)
            h = [extended(h_ref[r, c, p], 72 + (r * 3 + c) * PLANES + p) for c in range(3)]
            zero = jnp.zeros((ROWS, LANES), jnp.float32)
            e_up = (zero, zero) if p == PLANES - 1 else (up[1], up[2])
            new = next_magnetic(h, e, e_up, step, lanes)
            for c in range(3):
                ee_ref[r, c, p] = e[c]
                h1_ref[r, c, p] = new[c]
            up = e
        return carry

    lax.fori_loop(0, 3, per_real, 0)

    def per_plane(p, carry):
        for c in range(3):
            jj_ref[c, p] = extended(j_ref[c, p], 144 + c * PLANES + p)
        mm_ref[p] = extended(m_ref[p].astype(jnp.float32), 168 + p)
        return carry

    lax.fori_loop(0, PLANES, per_plane, 0)


def coefficients_of(density, mask, global_x, table, levels, lanes):
    m0, m1 = levels[0], levels[1]
    global_y = table[NARROW] * OWN + row_ids()
    inside = (
        (global_x >= table[BOX])
        & (global_x < table[BOX + 1])
        & (global_y >= table[BOX + 2])
        & (global_y < table[BOX + 3])
        & (lanes >= table[BOX + 4])
        & (lanes < table[BOX + 5])
    )
    in_grid = (
        (global_x >= 0)
        & (global_x < table[WIDE_COUNT] * PLANES)
        & (global_y >= 0)
        & (global_y < table[NARROW_COUNT] * OWN)
    )
    background = jnp.where(mask > 0.5, m1, m0)
    out = []
    for threshold in thresholds:
        base = float(np.tanh(sharpness * threshold))
        scale = 1.0 / (base + float(np.tanh(sharpness * (1.0 - threshold))))
        projected = (base + jnp.tanh(sharpness * (density - threshold))) * scale
        permittivity = jnp.where(inside, m0 + projected * (m1 - m0), background)
        out.append(jnp.where(in_grid, time_step / permittivity, 0.0))
    return out


def packed_halo(traces):
    rows = lax.broadcasted_iota(jnp.int32, (8, LANES), 0)
    tiles = []
    for c in range(2):
        halo = [traces[n][c][OWN:] for n in range(STEPS)]
        tiles.append(jnp.where(rows == 3, pltpu.roll(halo[3], 4, 0), halo[0]))
        tiles.append(jnp.where((rows > 1) & (rows < 5), pltpu.roll(halo[2], 4, 0), halo[1]))
    return tiles


def as_message(traces):
    tiles = []
    for n in range(STEPS):
        for c in range(2):
            tiles += [traces[n][c][8 * i : 8 * i + 8] for i in range(3)]
    return tiles + packed_halo(traces)


def from_message(tile):
    traces = []
    for n in range(STEPS):
        step = []
        for c in range(2):
            halo = tile(24 + 2 * c + (0 if n in (0, 3) else 1))
            halo = pltpu.roll(halo, 4, 0) if n > 1 else halo
            step.append(jnp.concatenate([tile((n * 2 + c) * 3 + i) for i in range(3)] + [halo], axis=0))
        traces.append(step)
    return traces


def trace_kernel(table, levels, g_ref, wz_ref, wy_ref, mm_ref, ee_ref, h1_ref, jj_ref, far_ref, near_ref, c_ref, d_ref):
    lanes = lane_ids()
    step = step_of_rows(table[NARROW])
    own, before, after = table[OWN_AT], table[BEFORE_AT], table[AFTER_AT]
    last = table[WIDE] == table[WIDE_COUNT] - 1
    coarse = [g_ref[before * 4 + 3]] + [g_ref[own * 4 + q] for q in range(4)]
    coarse.append(jnp.where(last, coarse[4], g_ref[after * 4]))
    coarse.append(g_ref[after * 4 + 1])
    along_z = jnp.dot(
        jnp.concatenate(coarse, axis=0),
        wz_ref[...],
        precision=lax.Precision.HIGHEST,
        preferred_element_type=jnp.float32,
    )
    strips = [
        jnp.concatenate([along_z[8 * q : 8 * q + 8, :LANES], along_z[8 * q : 8 * q + 8, LANES:]], axis=0)
        for q in range(7)
    ]
    along_y = jnp.dot(
        wy_ref[...],
        jnp.concatenate(strips, axis=1),
        precision=lax.Precision.HIGHEST,
        preferred_element_type=jnp.float32,
    )
    for q in range(7):
        d_ref[q] = along_y[:, LANES * q : LANES * (q + 1)]

    def own_plane(p, carry):
        q = 1 + lax.div(p, 2)
        lower = d_ref[q]
        upper = d_ref[q + lax.rem(p, 2)]
        values = coefficients_of(
            0.5 * (lower + upper), mm_ref[p], table[WIDE] * PLANES + p, table, levels, lanes
        )
        for r in range(3):
            c_ref[r, p] = values[r]
        return carry

    lax.fori_loop(0, PLANES, own_plane, 0)
    core = table[CORE]
    zero = jnp.zeros((ROWS, LANES), jnp.float32)

    def per_real(r, carry):
        def j(p):
            return [jj_ref[c, p] for c in range(3)]

        e = {p: [ee_ref[r, c, p] for c in range(3)] for p in (5, 6, 7)}
        h = {p: [h1_ref[r, c, p] for c in range(3)] for p in (4, 5, 6, 7)}
        up = [(h[7][1], h[7][2])]
        for first in (5, 6, 7):
            for p in range(first, 8):
                e[p] = next_electric(e[p], h[p], (h[p - 1][1], h[p - 1][2]), c_ref[r, p], j(p), lanes)
            e[8] = [zero] * 3
            for p in range(first, 8):
                h[p] = next_magnetic(h[p], e[p], (e[p + 1][1], e[p + 1][2]), step, lanes)
            up.append((h[7][1], h[7][2]))
        e = {p: [ee_ref[r, c, p] for c in range(3)] for p in (0, 1, 2)}
        h = {p: [h1_ref[r, c, p] for c in range(3)] for p in (0, 1, 2)}
        h[-1] = [zero] * 3
        down = [(e[0][1], e[0][2])]
        for last_plane in (2, 1, 0):
            for p in range(last_plane + 1):
                e[p] = next_electric(e[p], h[p], (h[p - 1][1], h[p - 1][2]), c_ref[r, p], j(p), lanes)
            down.append((e[0][1], e[0][2]))
            for p in range(last_plane):
                h[p] = next_magnetic(h[p], e[p], (e[p + 1][1], e[p + 1][2]), step, lanes)
        for i, (a, b) in enumerate(zip(as_message(up), as_message(down), strict=True)):
            far_ref[r * TILES + i] = jnp.where(core == 1, a, b)
            near_ref[r * TILES + i] = jnp.where(core == 1, b, a)
        return carry

    lax.fori_loop(0, 3, per_real, 0)


def ghost_kernel(table, levels, d_ref, far_ref, near_ref, c_ref):
    lanes = lane_ids()
    core = table[CORE]
    for i, (p, lower, upper) in enumerate(((-2, 0, 0), (-1, 0, 1), (8, 5, 5), (9, 5, 6))):
        far, near = far_ref[i % 2], near_ref[i % 2]
        mask = jnp.where(core == 0, far, near) if p < 0 else jnp.where(core == 1, far, near)
        values = coefficients_of(
            0.5 * (d_ref[lower] + d_ref[upper]), mask, table[WIDE] * PLANES + p, table, levels, lanes
        )
        for r in range(3):
            c_ref[r, i] = values[r]


def window_kernel(table, far_ref, near_ref, c_ref, g_ref, ee_ref, h1_ref, jj_ref, eo_ref, ho_ref):
    lanes = lane_ids()
    core = table[CORE]
    step = step_of_rows(table[NARROW])
    below = jnp.where(table[WIDE] == 0, 0.0, step)
    zero = jnp.zeros((ROWS, LANES), jnp.float32)

    def per_real(r, carry):
        def tile_from_below(i):
            return jnp.where(core == 0, far_ref[r * TILES + i], near_ref[r * TILES + i])

        def tile_from_above(i):
            return jnp.where(core == 1, far_ref[r * TILES + i], near_ref[r * TILES + i])

        trace_h = from_message(tile_from_below)
        trace_e = from_message(tile_from_above)

        def coefficient(p):
            if p < 0:
                return g_ref[r, p + 2]
            return g_ref[r, p - 6] if p >= PLANES else c_ref[r, p]

        def current(p):
            return [jj_ref[c, p] for c in range(3)] if 0 <= p < PLANES else None

        e = {p: [zero] * 3 for p in (-2, -1, 8, 9)}
        h = {p: [zero] * 3 for p in (-3, -2, -1, 8, 9)}
        for p in range(PLANES):
            e[p] = [ee_ref[r, c, p] for c in range(3)]
            h[p] = [h1_ref[r, c, p] for c in range(3)]
        h[7] = [h[7][0], h[7][1] + step * trace_e[0][1], h[7][2] - step * trace_e[0][0]]
        h[-1] = next_magnetic(h[-1], e[-1], (e[0][1], e[0][2]), below, lanes)

        def magnetic(planes, n):
            new = {}
            for p in planes:
                up = [e[p + 1][1], e[p + 1][2]]
                if p == 7:
                    up = [up[0] + trace_e[n - 1][0], up[1] + trace_e[n - 1][1]]
                new[p] = next_magnetic(h[p], e[p], up, below if p < 0 else step, lanes)
            h.update(new)

        def electric(planes, n):
            new = {}
            for p in planes:
                down = [h[p - 1][1], h[p - 1][2]]
                if p == 0:
                    down = [down[0] + trace_h[n - 1][0], down[1] + trace_h[n - 1][1]]
                new[p] = next_electric(e[p], h[p], down, coefficient(p), current(p), lanes)
            e.update(new)

        electric(range(-1, 9), 1)
        magnetic(range(-2, 9), 2)
        electric(range(-2, 10), 2)
        magnetic(range(-2, 9), 3)
        electric(range(-1, 9), 3)
        magnetic(range(-1, 8), 4)
        electric(range(8), 4)
        for p in range(PLANES):
            for c in range(3):
                eo_ref[r, c, p] = e[p][c][:OWN]
                ho_ref[r, c, p] = h[p][c][:OWN]
        return carry

    lax.fori_loop(0, 3, per_real, 0)


def refine_weights():
    along_z = np.zeros((64, LANES), np.float32)
    for cell in range(LANES):
        along_z[cell // 2, cell] += 0.5
        along_z[min((cell + 1) // 2, 63), cell] += 0.5
    both = np.zeros((LANES, 2 * LANES), np.float32)
    both[:64, :LANES] = along_z
    both[64:, LANES:] = along_z
    along_y = np.zeros((ROWS, 16), np.float32)
    for row in range(ROWS):
        y = row if row < OWN + HALO else row - ROWS
        along_y[row, y // 2 + 2] += 0.5
        along_y[row, min((y + 1) // 2 + 2, 15)] += 0.5
    return both, along_y


def call(kernel, outs, cost=None):
    return dict(
        out_shape=[jax.ShapeDtypeStruct(shape, jnp.float32) for shape in outs],
        out_specs=[pl.BlockSpec(memory_space=pltpu.VMEM) for _ in outs],
        compiler_params=pltpu.CompilerParams(vmem_limit_bytes=40 * 1024 * 1024),
        cost_estimate=cost,
        interpret=INTERPRET,
        name=kernel.__name__,
    )


def specs(smem, vmem):
    return [pl.BlockSpec(memory_space=pltpu.SMEM)] * smem + [pl.BlockSpec(memory_space=pltpu.VMEM)] * vmem


def body(
    electric,
    magnetic,
    current,
    density_tiles,
    tile_slabs,
    design_box,
    material_mask,
    material_levels,
):
    wide_count = lax.axis_size("wide")
    wide_place = lax.axis_index("wide")
    narrow_count = lax.axis_size("narrow")
    narrow_place = lax.axis_index("narrow")
    core = wide_place % 2
    half = wide_count // 2
    f32 = jnp.float32

    near_pairs = [(w, w ^ 1) for w in range(wide_count)]
    partner = [(w + 1) % wide_count if w % 2 else (w - 1) % wide_count for w in range(wide_count)]
    far_ring = [(w, partner[w]) for w in range(wide_count)]
    far_pairs = [(w, partner[w]) for w in range(1, wide_count - 1)]
    up = [(n, n + 1) for n in range(narrow_count - 1)]
    down = [(n + 1, n) for n in range(narrow_count - 1)]
    groups = [[w for w in range(wide_count) if (w // 2) % 2 == side] for side in range(2)]

    tile = density_tiles
    tile_lo = lax.ppermute(tile[:, 10:].reshape(4, 128), "narrow", up).reshape(4, 2, 64)
    tile_hi = lax.ppermute(tile[:, :2].reshape(4, 128), "narrow", down).reshape(4, 2, 64)
    tile_hi = jnp.where(narrow_place == narrow_count - 1, tile[:, 11:], tile_hi)
    rows = jnp.concatenate([tile_lo, tile, tile_hi], axis=1)
    packed = jnp.concatenate([rows[:, :8], rows[:, 8:]], axis=2)

    stack = [
        electric.reshape(72, OWN, LANES),
        magnetic.reshape(72, OWN, LANES),
        current.reshape(24, OWN, LANES),
        material_mask.astype(f32),
    ]
    first_rows = jnp.concatenate([x[:, :HALO] for x in stack], axis=0)
    last_rows = jnp.concatenate([x[:, OWN - HALO :] for x in stack], axis=0)
    low = lax.ppermute(last_rows, "narrow", up)
    high = lax.ppermute(first_rows, "narrow", down)

    other = lax.ppermute(packed, "wide", far_ring)
    held = jnp.concatenate([packed, other], axis=0)
    spread = jnp.broadcast_to(held, (half, 8, 8, LANES))
    gathered = lax.all_to_all(spread, "wide", 0, 0, axis_index_groups=groups, tiled=True)
    gathered = gathered.reshape(half * 8, 8, LANES)

    wanted = jnp.clip(wide_place + jnp.arange(-1, 2, dtype=jnp.int32), 0, wide_count - 1)
    ids = jnp.arange(wide_count, dtype=jnp.int32)
    at = jnp.sum(jnp.where(tile_slabs[None, :] == wanted[:, None], ids[None, :], 0), axis=1)
    mate = jnp.where(at % 2 == 1, at + 1, at - 1 + wide_count) % wide_count
    same_side = (at // 2) % 2 == (wide_place // 2) % 2
    holder = jnp.where(same_side, at, mate)
    place = ((holder // 4) * 2 + holder % 2) * 2 + jnp.where(same_side, 0, 1)
    table = jnp.concatenate(
        [
            jnp.stack([wide_place, narrow_place, core, jnp.int32(wide_count), jnp.int32(narrow_count)]),
            place[1:2],
            place[0:1],
            place[2:3],
            design_box,
        ]
    ).astype(jnp.int32)

    extended = (3, 3, PLANES, ROWS, LANES)
    planes = (PLANES, ROWS, LANES)
    e_ext, h_one, j_ext, m_ext = pl.pallas_call(
        extend_kernel,
        in_specs=specs(1, 6),
        **call(extend_kernel, [extended, extended, (3, *planes), planes]),
    )(table, electric, magnetic, current, material_mask, low, high)

    mask_up, mask_down = m_ext[6:], m_ext[:2]
    mask_far = lax.ppermute(jnp.where(core == 1, mask_up, mask_down), "wide", far_pairs)
    mask_near = lax.ppermute(jnp.where(core == 1, mask_down, mask_up), "wide", near_pairs)

    weights_z, weights_y = refine_weights()
    message = (3 * TILES, 8, LANES)
    far, near, own_c, dens = pl.pallas_call(
        trace_kernel,
        in_specs=specs(2, 7),
        **call(trace_kernel, [message, message, (3, *planes), (7, ROWS, LANES)]),
    )(table, material_levels, gathered, weights_z, weights_y, m_ext, e_ext, h_one, j_ext)

    near = lax.ppermute(near, "wide", near_pairs)
    far = lax.ppermute(far, "wide", far_pairs)

    (ghost_c,) = pl.pallas_call(
        ghost_kernel,
        in_specs=specs(2, 3),
        **call(ghost_kernel, [(3, 4, ROWS, LANES)]),
    )(table, material_levels, dens, mask_far, mask_near)

    own = (3, 3, PLANES, OWN, LANES)
    return tuple(
        pl.pallas_call(
            window_kernel,
            in_specs=specs(1, 7),
            **call(window_kernel, [own, own]),
        )(table, far, near, own_c, ghost_c, e_ext, h_one, j_ext)
    )


def solution(mesh):
    return jax.shard_map(
        body,
        mesh=mesh,
        in_specs=(
            P(None, None, "wide", "narrow", None),
            P(None, None, "wide", "narrow", None),
            P(None, "wide", "narrow", None),
            P("wide", "narrow", None),
            P(),
            P(),
            P("wide", "narrow", None),
            P(),
        ),
        out_specs=(P(None, None, "wide", "narrow", None), P(None, None, "wide", "narrow", None)),
        check_vma=False,
    )
```

```python
import jax
import jax.numpy as jnp
import numpy as np
from jax import lax
from jax.experimental import pallas as pl
from jax.experimental.pallas import tpu as pltpu
from jax.sharding import PartitionSpec as P

STEPS = 4
PLANES = 8
OWN = 24
ROWS = 32
HALO = 4
LANES = 128
FIRST_TILES = 8
COARSE = 6
TILES = 21

sharpness = 8.0
thresholds = (0.7, 0.5, 0.3)
time_step = 0.5

INTERPRET = False


def lane_ids():
    return lax.broadcasted_iota(jnp.int32, (ROWS, LANES), 1)


def row_ids():
    rows = lax.broadcasted_iota(jnp.int32, (ROWS, LANES), 0)
    return jnp.where(rows < OWN + HALO, rows, rows - ROWS)


def y_forward(a):
    return pltpu.roll(a, ROWS - 1, 0) - a


def y_backward(a):
    return a - pltpu.roll(a, 1, 0)


def z_forward(a, lanes):
    return jnp.where(lanes == LANES - 1, 0.0, pltpu.roll(a, LANES - 1, 1)) - a


def z_backward(a, lanes):
    return a - jnp.where(lanes == 0, 0.0, pltpu.roll(a, 1, 1))


def next_magnetic(h, e, e_up, step, lanes):
    up_y, up_z = e_up
    curl_x = y_forward(e[2]) - z_forward(e[1], lanes)
    curl_y = z_forward(e[0], lanes) - (up_z - e[2])
    curl_z = (up_y - e[1]) - y_forward(e[0])
    return [h[0] - step * curl_x, h[1] - step * curl_y, h[2] - step * curl_z]


def next_electric(e, h, h_down, coefficient, current, lanes):
    down_y, down_z = h_down
    curls = [
        y_backward(h[2]) - z_backward(h[1], lanes),
        z_backward(h[0], lanes) - (h[2] - down_z),
        (h[1] - down_y) - y_backward(h[0]),
    ]
    if current is not None:
        curls = [curls[c] - current[c] for c in range(3)]
    return [e[c] + coefficient * curls[c] for c in range(3)]


def step_of_rows(narrow_place):
    return jnp.where((row_ids() < 0) & (narrow_place == 0), 0.0, time_step)


WIDE, NARROW, CORE, WIDE_COUNT, NARROW_COUNT, BOX, MINE, THEIRS = 0, 1, 2, 3, 4, 5, 11, 17
E_AT, H_AT, J_AT, MASK_AT, HALO_PLANES = 0, 72, 144, 168, 176


def tiles_of(plane, count=4):
    return [plane[8 * i : 8 * i + 8] for i in range(count)]


def select(condition, yes, no):
    return [jnp.where(condition, a, b) for a, b in zip(yes, no, strict=True)]


def tile_rows_kernel(tile_ref, first_ref, last_ref):
    first_ref[...] = jnp.concatenate([tile_ref[0], tile_ref[1]], axis=1)
    last_ref[...] = jnp.concatenate([tile_ref[10], tile_ref[11]], axis=1)


def pack_kernel(e_first, e_last, h_first, h_last, j_first, j_last, m_first, m_last, first_ref, last_ref):
    for at, count, first, last in (
        (E_AT, 72, e_first, e_last),
        (H_AT, 72, h_first, h_last),
        (J_AT, 24, j_first, j_last),
        (MASK_AT, PLANES, m_first, m_last),
    ):
        first_ref[at : at + count] = first[:, :HALO].astype(jnp.float32)
        last_ref[at : at + count] = last[:, 8 - HALO :].astype(jnp.float32)


def tile_kernel(table, tile_ref, lo_ref, hi_ref, spread_ref):
    top = table[NARROW] == table[NARROW_COUNT] - 1
    for q in range(4):
        tile = jnp.concatenate([tile_ref[row, q : q + 1] for row in range(12)], axis=0)
        lo, hi = lo_ref[q : q + 1], hi_ref[q : q + 1]
        above = jnp.concatenate([hi[:, :64], hi[:, 64:]], axis=0)
        above = jnp.where(top, jnp.broadcast_to(tile[11:12], (2, 64)), above)
        first = jnp.concatenate([lo[:, :64], lo[:, 64:], tile[:6]], axis=0)
        second = jnp.concatenate([tile[6:], above], axis=0)
        packed = jnp.concatenate([first, second], axis=1)
        for i in range(spread_ref.shape[0]):
            spread_ref[i, q] = packed


def select_kernel(table, g_ref, message_ref, mine_ref, far_ref):
    for at, ref in ((MINE, mine_ref), (THEIRS, far_ref)):
        for i, (which, q) in enumerate(((0, 3), (1, 0), (1, 1), (1, 2), (1, 3), (2, 0))):
            held = g_ref[table[at + which] * 4 + q]
            ref[i] = jnp.where(table[at + 3 + which] == 1, held, 0.0)
    for i in range(3 * FIRST_TILES + 4):
        far_ref[COARSE + i] = message_ref[i]


def extend_kernel(
    table, e_ref, h_ref, j_ref, m_ref, lo_ref, hi_ref, ee_ref, h1_ref, jj_ref, mm_ref, far_ref, near_ref
):
    r = pl.program_id(0)
    lanes = lane_ids()
    step = step_of_rows(table[NARROW])
    core = table[CORE]
    zero = jnp.zeros((ROWS, LANES), jnp.float32)

    def extended(own, at):
        return jnp.concatenate([own, hi_ref[at], lo_ref[at]], axis=0)

    up = [zero] * 3
    upward = downward = None
    for p in range(PLANES - 1, -1, -1):
        at = r * 24 + p
        e = [extended(e_ref[0, c, p], E_AT + at + c * PLANES) for c in range(3)]
        h = [extended(h_ref[0, c, p], H_AT + at + c * PLANES) for c in range(3)]
        new = next_magnetic(h, e, (up[1], up[2]), step, lanes)
        for c in range(3):
            ee_ref[0, c, p] = e[c]
            h1_ref[0, c, p] = new[c]
        if p == PLANES - 1:
            upward = tiles_of(new[1]) + tiles_of(new[2])
        if p == 0:
            downward = tiles_of(e[1]) + tiles_of(e[2])
        up = e
    far, near = select(core == 1, upward, downward), select(core == 1, downward, upward)
    for i in range(FIRST_TILES):
        far_ref[r * FIRST_TILES + i] = far[i]
        near_ref[r * FIRST_TILES + i] = near[i]

    @pl.when(r == 0)
    def _():
        for p in range(PLANES):
            for c in range(3):
                jj_ref[c, p] = extended(j_ref[c, p], J_AT + c * PLANES + p)
            mm_ref[p] = extended(m_ref[p].astype(jnp.float32), MASK_AT + p)
        above, below = tiles_of(mm_ref[PLANES - 1]), tiles_of(mm_ref[0])
        far, near = select(core == 1, above, below), select(core == 1, below, above)
        for i in range(4):
            far_ref[3 * FIRST_TILES + i] = far[i]
            near_ref[3 * FIRST_TILES + i] = near[i]


def coefficients_of(density, mask, global_x, table, levels, lanes):
    m0, m1 = levels[0], levels[1]
    global_y = table[NARROW] * OWN + row_ids()
    inside = (
        (global_x >= table[BOX])
        & (global_x < table[BOX + 1])
        & (global_y >= table[BOX + 2])
        & (global_y < table[BOX + 3])
        & (lanes >= table[BOX + 4])
        & (lanes < table[BOX + 5])
    )
    in_grid = (
        (global_x >= 0)
        & (global_x < table[WIDE_COUNT] * PLANES)
        & (global_y >= 0)
        & (global_y < table[NARROW_COUNT] * OWN)
    )
    background = jnp.where(mask > 0.5, m1, m0)
    out = []
    for threshold in thresholds:
        base = float(np.tanh(sharpness * threshold))
        scale = 1.0 / (base + float(np.tanh(sharpness * (1.0 - threshold))))
        projected = (base + jnp.tanh(sharpness * (density - threshold))) * scale
        permittivity = jnp.where(inside, m0 + projected * (m1 - m0), background)
        out.append(jnp.where(in_grid, time_step / permittivity, 0.0))
    return out


def first_message(ref, at):
    return [jnp.concatenate([ref[at + 4 * c + i] for i in range(4)], axis=0) for c in range(2)]


def first_state(r, table, ee_ref, h1_ref, far_ref, near_ref, step):
    core = table[CORE]
    far, near = first_message(far_ref, COARSE + r * FIRST_TILES), first_message(near_ref, r * FIRST_TILES)
    trace_h = [jnp.where(table[WIDE] == 0, 0.0, x) for x in select(core == 0, far, near)]
    trace_e = [jnp.where(table[WIDE] == table[WIDE_COUNT] - 1, 0.0, x) for x in select(core == 1, far, near)]
    e = {p: [ee_ref[0, c, p] for c in range(3)] for p in range(PLANES)}
    h = {p: [h1_ref[0, c, p] for c in range(3)] for p in range(PLANES)}
    top = PLANES - 1
    h[top] = [h[top][0], h[top][1] + step * trace_e[1], h[top][2] - step * trace_e[0]]
    below = jnp.where(table[WIDE] == 0, 0.0, step)
    h[-1] = [None, trace_h[0] + below * e[0][2], trace_h[1] - below * e[0][1]]
    return e, h


def as_message(traces):
    rows = lax.broadcasted_iota(jnp.int32, (8, LANES), 0)
    tiles = []
    for n in range(3):
        for c in range(2):
            tiles += tiles_of(traces[n][c], 3)
    halo = [[traces[n][c][OWN:] for c in range(2)] for n in range(3)]
    for c in range(2):
        tiles.append(jnp.where((rows > 1) & (rows < 5), pltpu.roll(halo[1][c], 4, 0), halo[0][c]))
    tiles.append(jnp.where(rows == 3, pltpu.roll(halo[2][1], 4, 0), halo[2][0]))
    return tiles


def from_message(tile):
    traces = []
    for n in range(3):
        step = []
        for c in range(2):
            halo = tile(20) if n == 2 else tile(18 + c)
            halo = pltpu.roll(halo, 4, 0) if n == 1 or (n == 2 and c == 1) else halo
            step.append(jnp.concatenate([tile((n * 2 + c) * 3 + i) for i in range(3)] + [halo], axis=0))
        traces.append(step)
    return traces


def refine(table, mine_ref, far_ref, wz_ref, wy_ref, d_ref):
    last = table[WIDE] == table[WIDE_COUNT] - 1
    coarse = [mine_ref[q] + far_ref[q] for q in range(COARSE)]
    coarse[5] = jnp.where(last, coarse[4], coarse[5])
    along_z = jnp.dot(
        jnp.concatenate(coarse, axis=0),
        wz_ref[...],
        precision=lax.Precision.HIGHEST,
        preferred_element_type=jnp.float32,
    )
    strips = [
        jnp.concatenate([along_z[8 * q : 8 * q + 8, :LANES], along_z[8 * q : 8 * q + 8, LANES:]], axis=0)
        for q in range(COARSE)
    ]
    along_y = jnp.dot(
        wy_ref[...],
        jnp.concatenate(strips, axis=1),
        precision=lax.Precision.HIGHEST,
        preferred_element_type=jnp.float32,
    )
    for q in range(COARSE):
        d_ref[q] = along_y[:, LANES * q : LANES * (q + 1)]


def plane_coefficients(p, mask, table, levels, d_ref, c_ref):
    q = 1 + p // 2
    density = d_ref[q] if p % 2 == 0 else 0.5 * (d_ref[q] + d_ref[q + 1])
    values = coefficients_of(density, mask, table[WIDE] * PLANES + p, table, levels, lane_ids())
    for r in range(3):
        c_ref[r, p + 1] = values[r]


def trace_kernel(
    table, levels, mine_ref, wz_ref, wy_ref, mm_ref, far_ref, near_ref, ee_ref, h1_ref, jj_ref,
    far_out, near_out, c_ref, d_ref,
):
    r = pl.program_id(0)

    @pl.when(r == 0)
    def _():
        refine(table, mine_ref, far_ref, wz_ref, wy_ref, d_ref)
        for p in (0, 1, 2, 5, 6, 7):
            plane_coefficients(p, mm_ref[p], table, levels, d_ref, c_ref)

    lanes = lane_ids()
    step = step_of_rows(table[NARROW])
    core = table[CORE]
    zero = jnp.zeros((ROWS, LANES), jnp.float32)
    e, h = first_state(r, table, ee_ref, h1_ref, far_ref, near_ref, step)

    def electric(p):
        current = [jj_ref[c, p] for c in range(3)]
        e[p] = next_electric(e[p], h[p], (h[p - 1][1], h[p - 1][2]), c_ref[r, p + 1], current, lanes)

    def magnetic(p):
        h[p] = next_magnetic(h[p], e[p], (e[p + 1][1], e[p + 1][2]), step, lanes)

    for p in (0, 1, 2, 5, 6, 7):
        electric(p)
    h[-1] = [zero] * 3
    e[8] = [zero] * 3
    upward, downward = [], [(e[0][1], e[0][2])]
    for first in (5, 6, 7):
        for p in range(first, 8):
            magnetic(p)
        upward.append((h[7][1], h[7][2]))
        for p in range(first + 1, 8):
            electric(p)
    for last_plane in (1, 0):
        for p in range(last_plane + 1):
            magnetic(p)
        for p in range(last_plane + 1):
            electric(p)
        downward.append((e[0][1], e[0][2]))
    for i, (a, b) in enumerate(zip(as_message(upward), as_message(downward), strict=True)):
        far_out[r * TILES + i] = jnp.where(core == 1, a, b)
        near_out[r * TILES + i] = jnp.where(core == 1, b, a)


def inner_kernel(
    table, levels, mine_ref, wz_ref, wy_ref, mm_ref, far_ref, near_ref, ee_ref, h1_ref, jj_ref,
    eo_ref, ho_ref, c_ref, d_ref,
):
    r = pl.program_id(0)

    @pl.when(r == 0)
    def _():
        refine(table, mine_ref, far_ref, wz_ref, wy_ref, d_ref)
        core = table[CORE]
        far = jnp.concatenate([far_ref[COARSE + 3 * FIRST_TILES + i] for i in range(4)], axis=0)
        near = jnp.concatenate([near_ref[3 * FIRST_TILES + i] for i in range(4)], axis=0)
        for p in range(-1, PLANES + 1):
            if p < 0:
                mask = jnp.where(core == 0, far, near)
            else:
                mask = mm_ref[p] if p < PLANES else jnp.where(core == 1, far, near)
            plane_coefficients(p, mask, table, levels, d_ref, c_ref)

    lanes = lane_ids()
    step = step_of_rows(table[NARROW])
    e, h = first_state(r, table, ee_ref, h1_ref, far_ref, near_ref, step)

    def electric(first, last):
        for p in range(first, last + 1):
            current = [jj_ref[c, p] for c in range(3)]
            e[p] = next_electric(e[p], h[p], (h[p - 1][1], h[p - 1][2]), c_ref[r, p + 1], current, lanes)

    def magnetic(first, last):
        for p in range(first, last + 1):
            h[p] = next_magnetic(h[p], e[p], (e[p + 1][1], e[p + 1][2]), step, lanes)

    electric(0, 7)
    magnetic(0, 6)
    electric(1, 6)
    magnetic(1, 5)
    electric(2, 5)
    magnetic(2, 4)
    electric(3, 4)
    for p in range(PLANES):
        for c in range(3):
            eo_ref[0, c, p] = e[p][c]
            ho_ref[0, c, p] = h[p][c]


def window_kernel(table, c_ref, far_ref, near_ref, ee_ref, hh_ref, jj_ref, eo_ref, ho_ref):
    r = pl.program_id(0)
    lanes = lane_ids()
    core = table[CORE]
    step = step_of_rows(table[NARROW])
    below = jnp.where(table[WIDE] == 0, 0.0, step)
    zero = jnp.zeros((ROWS, LANES), jnp.float32)

    def tile_from_below(i):
        return jnp.where(core == 0, far_ref[r * TILES + i], near_ref[r * TILES + i])

    def tile_from_above(i):
        return jnp.where(core == 1, far_ref[r * TILES + i], near_ref[r * TILES + i])

    trace_h = from_message(tile_from_below)
    trace_e = from_message(tile_from_above)
    e = {p: [zero] * 3 for p in (-2, -1, 8, 9)}
    h = {p: [zero] * 3 for p in (-2, -1, 8)}
    for p in range(PLANES):
        e[p] = [ee_ref[0, c, p] for c in range(3)]
        h[p] = [hh_ref[0, c, p] for c in range(3)]

    def magnetic(planes, n):
        for p in planes:
            up = [e[p + 1][1], e[p + 1][2]]
            if p == 7:
                up = [up[0] + trace_e[n - 2][0], up[1] + trace_e[n - 2][1]]
            h[p] = next_magnetic(h[p], e[p], up, below if p < 0 else step, lanes)

    def electric(planes, n):
        for p in planes:
            down = [h[p - 1][1], h[p - 1][2]]
            if p == 0:
                down = [down[0] + trace_h[n - 2][0], down[1] + trace_h[n - 2][1]]
            current = [jj_ref[c, p] for c in range(3)] if 0 <= p < PLANES else None
            e[p] = next_electric(e[p], h[p], down, c_ref[0, p + 1], current, lanes)

    magnetic((-1, 7), 2)
    electric((0, 7, 8), 2)
    e[-1] = next_electric(e[-1], h[-1], (zero, zero), c_ref[0, 0], None, lanes)
    magnetic((-2, -1, 0, 6, 7, 8), 3)
    electric((-1, 0, 1, 6, 7, 8), 3)
    magnetic((-1, 0, 1, 5, 6, 7), 4)
    electric((0, 1, 2, 5, 6, 7), 4)
    for p in range(PLANES):
        for c in range(3):
            eo_ref[0, c, p] = e[p][c][:OWN]
            ho_ref[0, c, p] = h[p][c][:OWN]


def refine_weights():
    along_z = np.zeros((64, LANES), np.float32)
    for cell in range(LANES):
        along_z[cell // 2, cell] += 0.5
        along_z[min((cell + 1) // 2, 63), cell] += 0.5
    both = np.zeros((LANES, 2 * LANES), np.float32)
    both[:64, :LANES] = along_z
    both[64:, LANES:] = along_z
    along_y = np.zeros((ROWS, 16), np.float32)
    for row in range(ROWS):
        y = row if row < OWN + HALO else row - ROWS
        along_y[row, y // 2 + 2] += 0.5
        along_y[row, min((y + 1) // 2 + 2, 15)] += 0.5
    return both, along_y


def run(kernel, scalars, operands, outs, flops, scratch=(), steps=3, limit=60):
    def spec(shape, block):
        rank = len(shape)
        if block is None:
            return pl.BlockSpec(tuple(shape), lambda r: (0,) * rank)
        if block is True:
            return pl.BlockSpec((1, *shape[1:]), lambda r: (r,) + (0,) * (rank - 1))
        block_shape, place = block
        return pl.BlockSpec(block_shape, lambda r: place)

    moved = sum(4 * int(np.prod(x.shape)) for x, _ in operands) + sum(4 * int(np.prod(x)) for x, _ in outs)
    return pl.pallas_call(
        kernel,
        grid=(steps,),
        in_specs=[pl.BlockSpec(memory_space=pltpu.SMEM)] * len(scalars)
        + [spec(x.shape, block) for x, block in operands],
        out_specs=[spec(shape, block) for shape, block in outs],
        out_shape=[jax.ShapeDtypeStruct(shape, jnp.float32) for shape, _ in outs],
        scratch_shapes=list(scratch),
        compiler_params=pltpu.CompilerParams(
            dimension_semantics=("arbitrary",), vmem_limit_bytes=limit * 1024 * 1024
        ),
        cost_estimate=pl.CostEstimate(flops=flops, bytes_accessed=moved, transcendentals=0),
        interpret=INTERPRET,
        name=kernel.__name__,
    )(*scalars, *[x for x, _ in operands])


def body(
    electric,
    magnetic,
    current,
    density_tiles,
    tile_slabs,
    design_box,
    material_mask,
    material_levels,
):
    wide_count = lax.axis_size("wide")
    wide_place = lax.axis_index("wide")
    narrow_count = lax.axis_size("narrow")
    narrow_place = lax.axis_index("narrow")
    core = wide_place % 2
    half = wide_count // 2

    near_pairs = [(w, w ^ 1) for w in range(wide_count)]
    partner = [(w + 1) % wide_count if w % 2 else (w - 1) % wide_count for w in range(wide_count)]
    far_ring = [(w, partner[w]) for w in range(wide_count)]
    far_pairs = [(w, partner[w]) for w in range(1, wide_count - 1)]
    up = [(n, n + 1) for n in range(narrow_count - 1)]
    down = [(n + 1, n) for n in range(narrow_count - 1)]
    groups = [[w for w in range(wide_count) if (w // 2) % 2 == side] for side in range(2)]

    mate = jnp.where(wide_place % 2 == 1, wide_place + 1, wide_place - 1 + wide_count) % wide_count
    slabs = jnp.stack([wide_place, mate])[:, None] + jnp.arange(-1, 2, dtype=jnp.int32)[None, :]
    slabs = jnp.clip(slabs, 0, wide_count - 1)
    ids = jnp.arange(wide_count, dtype=jnp.int32)
    at = jnp.sum(jnp.where(tile_slabs[None, None, :] == slabs[:, :, None], ids, 0), axis=2)
    here = ((at // 2) % 2 == (wide_place // 2) % 2).astype(jnp.int32)
    place = (at // 4) * 2 + at % 2
    table = jnp.concatenate(
        [
            jnp.stack([wide_place, narrow_place, core, jnp.int32(wide_count), jnp.int32(narrow_count)]),
            design_box,
            jnp.stack([place, here], axis=1).reshape(12),
        ]
    ).astype(jnp.int32)

    stack = [
        electric.reshape(72, OWN, LANES),
        magnetic.reshape(72, OWN, LANES),
        current.reshape(24, OWN, LANES),
        material_mask,
    ]
    ends = [(x, ((x.shape[0], 8, LANES), (0, row, 0))) for x in stack for row in (0, 2)]
    halo = (HALO_PLANES, HALO, LANES)
    first_rows, last_rows = run(pack_kernel, (), ends, [(halo, None), (halo, None)], 1_000_000, steps=1)
    tile = jnp.transpose(density_tiles, (1, 0, 2))
    tile_first, tile_last = run(
        tile_rows_kernel, (), [(tile, None)], [((4, LANES), None), ((4, LANES), None)], 1000, steps=1, limit=8
    )
    tile_lo = lax.ppermute(tile_last, "narrow", up)
    tile_hi = lax.ppermute(tile_first, "narrow", down)
    early, first_rows, last_rows = lax.optimization_barrier((table, first_rows, last_rows))
    (spread,) = run(
        tile_kernel,
        (early,),
        [(tile, None), (tile_lo, None), (tile_hi, None)],
        [((half, 4, 8, LANES), None)],
        1_000_000,
        steps=1,
        limit=8,
    )
    gathered = lax.all_to_all(spread, "wide", 0, 0, axis_index_groups=groups, tiled=True)
    gathered = gathered.reshape(half * 4, 8, LANES)

    low = lax.ppermute(last_rows, "narrow", up)
    high = lax.ppermute(first_rows, "narrow", down)

    extended = (3, 3, PLANES, ROWS, LANES)
    planes = (PLANES, ROWS, LANES)
    message = (3 * FIRST_TILES + 4, 8, LANES)
    e_ext, h_one, j_ext, m_ext, far, near = run(
        extend_kernel,
        (table,),
        [(electric, True), (magnetic, True), (current, None), (material_mask, None), (low, None), (high, None)],
        [(extended, True), (extended, True), ((3, *planes), None), (planes, None), (message, None), (message, None)],
        10_000_000,
    )
    near = lax.ppermute(near, "wide", near_pairs)

    mine, far = run(
        select_kernel,
        (table,),
        [(gathered, None), (far, None)],
        [((COARSE, 8, LANES), None), ((COARSE + message[0], 8, LANES), None)],
        1_000_000,
        steps=1,
        limit=8,
    )
    far = lax.ppermute(far, "wide", far_ring)
    fields = [(e_ext, True), (h_one, True), (j_ext, None)]

    weights_z, weights_y = refine_weights()
    message = (3 * TILES, 8, LANES)
    coefficients = (3, PLANES + 2, ROWS, LANES)
    strips = pltpu.VMEM((COARSE, ROWS, LANES), jnp.float32)
    inputs = [(x, None) for x in (mine, weights_z, weights_y, m_ext, far, near)] + fields
    far_end, near_end = run(
        trace_kernel,
        (table, material_levels),
        inputs,
        [(message, None), (message, None)],
        10_000_000,
        [pltpu.VMEM(coefficients, jnp.float32), strips],
    )
    near_end = lax.ppermute(near_end, "wide", near_pairs)
    far_end = lax.ppermute(far_end, "wide", far_pairs)

    e_in, h_in, coefficient = run(
        inner_kernel,
        (table, material_levels),
        inputs,
        [(extended, True), (extended, True), (coefficients, None)],
        10_000_000,
        [strips],
        limit=24,
    )
    own = (3, 3, PLANES, OWN, LANES)
    return tuple(
        run(
            window_kernel,
            (table,),
            [(coefficient, True), (far_end, None), (near_end, None), (e_in, True), (h_in, True), (j_ext, None)],
            [(own, True), (own, True)],
            10_000_000,
            limit=24,
        )
    )


def solution(mesh):
    return jax.shard_map(
        body,
        mesh=mesh,
        in_specs=(
            P(None, None, "wide", "narrow", None),
            P(None, None, "wide", "narrow", None),
            P(None, "wide", "narrow", None),
            P("wide", "narrow", None),
            P(),
            P(),
            P("wide", "narrow", None),
            P(),
        ),
        out_specs=(P(None, None, "wide", "narrow", None), P(None, None, "wide", "narrow", None)),
        check_vma=False,
    )
```

```python
import jax
import jax.numpy as jnp
import numpy as np
from jax import lax
from jax.experimental import pallas as pl
from jax.experimental.pallas import tpu as pltpu
from jax.sharding import PartitionSpec as P

STEPS = 4
PLANES = 8
OWN = 24
ROWS = 32
HALO = 4
LANES = 128
FIRST_TILES = 8
COARSE = 6
TILES = 21

sharpness = 8.0
thresholds = (0.7, 0.5, 0.3)
time_step = 0.5

INTERPRET = False


def lane_ids():
    return lax.broadcasted_iota(jnp.int32, (ROWS, LANES), 1)


def row_ids():
    rows = lax.broadcasted_iota(jnp.int32, (ROWS, LANES), 0)
    return jnp.where(rows < OWN + HALO, rows, rows - ROWS)


def y_forward(a):
    return pltpu.roll(a, ROWS - 1, 0) - a


def y_backward(a):
    return a - pltpu.roll(a, 1, 0)


def z_forward(a, lanes):
    return jnp.where(lanes == LANES - 1, 0.0, pltpu.roll(a, LANES - 1, 1)) - a


def z_backward(a, lanes):
    return a - jnp.where(lanes == 0, 0.0, pltpu.roll(a, 1, 1))


def next_magnetic(h, e, e_up, step, lanes):
    up_y, up_z = e_up
    curl_x = y_forward(e[2]) - z_forward(e[1], lanes)
    curl_y = z_forward(e[0], lanes) - (up_z - e[2])
    curl_z = (up_y - e[1]) - y_forward(e[0])
    return [h[0] - step * curl_x, h[1] - step * curl_y, h[2] - step * curl_z]


def next_electric(e, h, h_down, coefficient, current, lanes):
    down_y, down_z = h_down
    curls = [
        y_backward(h[2]) - z_backward(h[1], lanes),
        z_backward(h[0], lanes) - (h[2] - down_z),
        (h[1] - down_y) - y_backward(h[0]),
    ]
    if current is not None:
        curls = [curls[c] - current[c] for c in range(3)]
    return [e[c] + coefficient * curls[c] for c in range(3)]


def step_of_rows(narrow_place):
    return jnp.where((row_ids() < 0) & (narrow_place == 0), 0.0, time_step)


WIDE, NARROW, CORE, WIDE_COUNT, NARROW_COUNT, BOX, MINE, THEIRS = 0, 1, 2, 3, 4, 5, 11, 17
E_AT, H_AT, J_AT, MASK_AT, HALO_PLANES = 0, 72, 144, 168, 176


def tiles_of(plane, count=4):
    return [plane[8 * i : 8 * i + 8] for i in range(count)]


def select(condition, yes, no):
    return [jnp.where(condition, a, b) for a, b in zip(yes, no, strict=True)]


def tile_rows_kernel(tile_ref, first_ref, last_ref):
    first_ref[...] = jnp.concatenate([tile_ref[0], tile_ref[1]], axis=1)
    last_ref[...] = jnp.concatenate([tile_ref[10], tile_ref[11]], axis=1)


def pack_kernel(e_first, e_last, h_first, h_last, j_first, j_last, m_first, m_last, first_ref, last_ref):
    for at, count, first, last in (
        (E_AT, 72, e_first, e_last),
        (H_AT, 72, h_first, h_last),
        (J_AT, 24, j_first, j_last),
        (MASK_AT, PLANES, m_first, m_last),
    ):
        first_ref[at : at + count] = first[:, :HALO].astype(jnp.float32)
        last_ref[at : at + count] = last[:, 8 - HALO :].astype(jnp.float32)


def tile_kernel(table, tile_ref, lo_ref, hi_ref, spread_ref):
    top = table[NARROW] == table[NARROW_COUNT] - 1
    for q in range(4):
        tile = jnp.concatenate([tile_ref[row, q : q + 1] for row in range(12)], axis=0)
        lo, hi = lo_ref[q : q + 1], hi_ref[q : q + 1]
        above = jnp.concatenate([hi[:, :64], hi[:, 64:]], axis=0)
        above = jnp.where(top, jnp.broadcast_to(tile[11:12], (2, 64)), above)
        first = jnp.concatenate([lo[:, :64], lo[:, 64:], tile[:6]], axis=0)
        second = jnp.concatenate([tile[6:], above], axis=0)
        packed = jnp.concatenate([first, second], axis=1)
        for i in range(spread_ref.shape[0]):
            spread_ref[i, q] = packed


def select_kernel(table, g_ref, message_ref, mine_ref, far_ref, sem):
    copy = pltpu.make_async_copy(message_ref, far_ref.at[pl.ds(COARSE, 3 * FIRST_TILES + 4)], sem)
    copy.start()
    for at, ref in ((MINE, mine_ref), (THEIRS, far_ref)):
        for i, (which, q) in enumerate(((0, 3), (1, 0), (1, 1), (1, 2), (1, 3), (2, 0))):
            held = g_ref[table[at + which] * 4 + q]
            ref[i] = jnp.where(table[at + 3 + which] == 1, held, 0.0)
    copy.wait()


def extend_kernel(
    table, e_ref, h_ref, j_ref, m_ref, lo_ref, hi_ref, ee_ref, h1_ref, jj_ref, mm_ref, far_ref, near_ref
):
    r = pl.program_id(0)
    lanes = lane_ids()
    step = step_of_rows(table[NARROW])
    core = table[CORE]
    zero = jnp.zeros((ROWS, LANES), jnp.float32)

    def extended(own, at):
        return jnp.concatenate([own, hi_ref[at], lo_ref[at]], axis=0)

    up = [zero] * 3
    upward = downward = None
    for p in range(PLANES - 1, -1, -1):
        at = r * 24 + p
        e = [extended(e_ref[0, c, p], E_AT + at + c * PLANES) for c in range(3)]
        h = [extended(h_ref[0, c, p], H_AT + at + c * PLANES) for c in range(3)]
        new = next_magnetic(h, e, (up[1], up[2]), step, lanes)
        for c in range(3):
            ee_ref[0, c, p] = e[c]
            h1_ref[0, c, p] = new[c]
        if p == PLANES - 1:
            upward = tiles_of(new[1]) + tiles_of(new[2])
        if p == 0:
            downward = tiles_of(e[1]) + tiles_of(e[2])
        up = e
    far, near = select(core == 1, upward, downward), select(core == 1, downward, upward)
    for i in range(FIRST_TILES):
        far_ref[r * FIRST_TILES + i] = far[i]
        near_ref[r * FIRST_TILES + i] = near[i]

    @pl.when(r == 0)
    def _():
        for p in range(PLANES):
            for c in range(3):
                jj_ref[c, p] = extended(j_ref[c, p], J_AT + c * PLANES + p)
            mm_ref[p] = extended(m_ref[p].astype(jnp.float32), MASK_AT + p)
        above, below = tiles_of(mm_ref[PLANES - 1]), tiles_of(mm_ref[0])
        far, near = select(core == 1, above, below), select(core == 1, below, above)
        for i in range(4):
            far_ref[3 * FIRST_TILES + i] = far[i]
            near_ref[3 * FIRST_TILES + i] = near[i]


def coefficients_of(density, mask, global_x, table, levels, lanes):
    m0, m1 = levels[0], levels[1]
    global_y = table[NARROW] * OWN + row_ids()
    inside = (
        (global_x >= table[BOX])
        & (global_x < table[BOX + 1])
        & (global_y >= table[BOX + 2])
        & (global_y < table[BOX + 3])
        & (lanes >= table[BOX + 4])
        & (lanes < table[BOX + 5])
    )
    in_grid = (
        (global_x >= 0)
        & (global_x < table[WIDE_COUNT] * PLANES)
        & (global_y >= 0)
        & (global_y < table[NARROW_COUNT] * OWN)
    )
    background = jnp.where(mask > 0.5, m1, m0)
    out = []
    for threshold in thresholds:
        base = float(np.tanh(sharpness * threshold))
        scale = 1.0 / (base + float(np.tanh(sharpness * (1.0 - threshold))))
        projected = (base + jnp.tanh(sharpness * (density - threshold))) * scale
        permittivity = jnp.where(inside, m0 + projected * (m1 - m0), background)
        out.append(jnp.where(in_grid, time_step / permittivity, 0.0))
    return out


def first_message(ref, at):
    return [jnp.concatenate([ref[at + 4 * c + i] for i in range(4)], axis=0) for c in range(2)]


def first_state(r, block, table, ee_ref, h1_ref, far_ref, near_ref, step):
    core = table[CORE]
    far, near = first_message(far_ref, COARSE + r * FIRST_TILES), first_message(near_ref, r * FIRST_TILES)
    trace_h = [jnp.where(table[WIDE] == 0, 0.0, x) for x in select(core == 0, far, near)]
    trace_e = [jnp.where(table[WIDE] == table[WIDE_COUNT] - 1, 0.0, x) for x in select(core == 1, far, near)]
    e = {p: [ee_ref[block, c, p] for c in range(3)] for p in range(PLANES)}
    h = {p: [h1_ref[block, c, p] for c in range(3)] for p in range(PLANES)}
    top = PLANES - 1
    h[top] = [h[top][0], h[top][1] + step * trace_e[1], h[top][2] - step * trace_e[0]]
    below = jnp.where(table[WIDE] == 0, 0.0, step)
    h[-1] = [None, trace_h[0] + below * e[0][2], trace_h[1] - below * e[0][1]]
    return e, h


def as_message(traces):
    rows = lax.broadcasted_iota(jnp.int32, (8, LANES), 0)
    tiles = []
    for n in range(3):
        for c in range(2):
            tiles += tiles_of(traces[n][c], 3)
    halo = [[traces[n][c][OWN:] for c in range(2)] for n in range(3)]
    for c in range(2):
        tiles.append(jnp.where((rows > 1) & (rows < 5), pltpu.roll(halo[1][c], 4, 0), halo[0][c]))
    tiles.append(jnp.where(rows == 3, pltpu.roll(halo[2][1], 4, 0), halo[2][0]))
    return tiles


def from_message(tile):
    traces = []
    for n in range(3):
        step = []
        for c in range(2):
            halo = tile(20) if n == 2 else tile(18 + c)
            halo = pltpu.roll(halo, 4, 0) if n == 1 or (n == 2 and c == 1) else halo
            step.append(jnp.concatenate([tile((n * 2 + c) * 3 + i) for i in range(3)] + [halo], axis=0))
        traces.append(step)
    return traces


def refine(table, mine_ref, far_ref, wz_ref, wy_ref, d_ref):
    last = table[WIDE] == table[WIDE_COUNT] - 1
    coarse = [mine_ref[q] + far_ref[q] for q in range(COARSE)]
    coarse[5] = jnp.where(last, coarse[4], coarse[5])
    along_z = jnp.dot(
        jnp.concatenate(coarse, axis=0),
        wz_ref[...],
        precision=lax.Precision.HIGHEST,
        preferred_element_type=jnp.float32,
    )
    strips = [
        jnp.concatenate([along_z[8 * q : 8 * q + 8, :LANES], along_z[8 * q : 8 * q + 8, LANES:]], axis=0)
        for q in range(COARSE)
    ]
    along_y = jnp.dot(
        wy_ref[...],
        jnp.concatenate(strips, axis=1),
        precision=lax.Precision.HIGHEST,
        preferred_element_type=jnp.float32,
    )
    for q in range(COARSE):
        d_ref[q] = along_y[:, LANES * q : LANES * (q + 1)]


def plane_coefficients(p, mask, table, levels, d_ref, c_ref):
    q = 1 + p // 2
    density = d_ref[q] if p % 2 == 0 else 0.5 * (d_ref[q] + d_ref[q + 1])
    values = coefficients_of(density, mask, table[WIDE] * PLANES + p, table, levels, lane_ids())
    for r in range(3):
        c_ref[r, p + 1] = values[r]


def trace_kernel(
    table, levels, mine_ref, wz_ref, wy_ref, mm_ref, far_ref, near_ref, ee_ref, h1_ref, jj_ref,
    far_out, near_out, c_ref, d_ref,
):
    refine(table, mine_ref, far_ref, wz_ref, wy_ref, d_ref)
    for p in (0, 1, 2, 5, 6, 7):
        plane_coefficients(p, mm_ref[p], table, levels, d_ref, c_ref)
    lanes = lane_ids()
    step = step_of_rows(table[NARROW])
    core = table[CORE]
    zero = jnp.zeros((ROWS, LANES), jnp.float32)

    def per_real(r, carry):
        e, h = first_state(r, r, table, ee_ref, h1_ref, far_ref, near_ref, step)

        def electric(p):
            current = [jj_ref[c, p] for c in range(3)]
            e[p] = next_electric(e[p], h[p], (h[p - 1][1], h[p - 1][2]), c_ref[r, p + 1], current, lanes)

        def magnetic(p):
            h[p] = next_magnetic(h[p], e[p], (e[p + 1][1], e[p + 1][2]), step, lanes)

        for p in (0, 1, 2, 5, 6, 7):
            electric(p)
        h[-1] = [zero] * 3
        e[8] = [zero] * 3
        upward, downward = [], [(e[0][1], e[0][2])]
        for first in (5, 6, 7):
            for p in range(first, 8):
                magnetic(p)
            upward.append((h[7][1], h[7][2]))
            for p in range(first + 1, 8):
                electric(p)
        for last_plane in (1, 0):
            for p in range(last_plane + 1):
                magnetic(p)
            for p in range(last_plane + 1):
                electric(p)
            downward.append((e[0][1], e[0][2]))
        for i, (a, b) in enumerate(zip(as_message(upward), as_message(downward), strict=True)):
            far_out[r * TILES + i] = jnp.where(core == 1, a, b)
            near_out[r * TILES + i] = jnp.where(core == 1, b, a)
        return carry

    lax.fori_loop(0, 3, per_real, 0)


def stage_kernel(*refs):
    for source, copied in zip(refs[: len(refs) // 2], refs[len(refs) // 2 :], strict=True):
        copied[...] = source[...]


def inner_kernel(
    table, levels, mine_ref, wz_ref, wy_ref, mm_ref, far_ref, near_ref, ee_ref, h1_ref, jj_ref,
    eo_ref, ho_ref, c_ref, d_ref,
):
    r = pl.program_id(0)

    @pl.when(r == 0)
    def _():
        refine(table, mine_ref, far_ref, wz_ref, wy_ref, d_ref)
        core = table[CORE]
        far = jnp.concatenate([far_ref[COARSE + 3 * FIRST_TILES + i] for i in range(4)], axis=0)
        near = jnp.concatenate([near_ref[3 * FIRST_TILES + i] for i in range(4)], axis=0)
        for p in range(-1, PLANES + 1):
            if p < 0:
                mask = jnp.where(core == 0, far, near)
            else:
                mask = mm_ref[p] if p < PLANES else jnp.where(core == 1, far, near)
            plane_coefficients(p, mask, table, levels, d_ref, c_ref)

    lanes = lane_ids()
    step = step_of_rows(table[NARROW])
    e, h = first_state(r, 0, table, ee_ref, h1_ref, far_ref, near_ref, step)

    def electric(first, last):
        for p in range(first, last + 1):
            current = [jj_ref[c, p] for c in range(3)]
            e[p] = next_electric(e[p], h[p], (h[p - 1][1], h[p - 1][2]), c_ref[r, p + 1], current, lanes)

    def magnetic(first, last):
        for p in range(first, last + 1):
            h[p] = next_magnetic(h[p], e[p], (e[p + 1][1], e[p + 1][2]), step, lanes)

    electric(0, 7)
    magnetic(0, 6)
    electric(1, 6)
    magnetic(1, 5)
    electric(2, 5)
    magnetic(2, 4)
    electric(3, 4)
    for p in range(PLANES):
        for c in range(3):
            eo_ref[0, c, p] = e[p][c]
            ho_ref[0, c, p] = h[p][c]


def window_kernel(table, c_ref, far_ref, near_ref, ee_ref, hh_ref, jj_ref, eo_ref, ho_ref):
    r = pl.program_id(0)
    lanes = lane_ids()
    core = table[CORE]
    step = step_of_rows(table[NARROW])
    below = jnp.where(table[WIDE] == 0, 0.0, step)
    zero = jnp.zeros((ROWS, LANES), jnp.float32)

    def tile_from_below(i):
        return jnp.where(core == 0, far_ref[r * TILES + i], near_ref[r * TILES + i])

    def tile_from_above(i):
        return jnp.where(core == 1, far_ref[r * TILES + i], near_ref[r * TILES + i])

    trace_h = from_message(tile_from_below)
    trace_e = from_message(tile_from_above)
    e = {p: [zero] * 3 for p in (-2, -1, 8, 9)}
    h = {p: [zero] * 3 for p in (-2, -1, 8)}
    for p in range(PLANES):
        e[p] = [ee_ref[0, c, p] for c in range(3)]
        h[p] = [hh_ref[0, c, p] for c in range(3)]

    def magnetic(planes, n):
        for p in planes:
            up = [e[p + 1][1], e[p + 1][2]]
            if p == 7:
                up = [up[0] + trace_e[n - 2][0], up[1] + trace_e[n - 2][1]]
            h[p] = next_magnetic(h[p], e[p], up, below if p < 0 else step, lanes)

    def electric(planes, n):
        for p in planes:
            down = [h[p - 1][1], h[p - 1][2]]
            if p == 0:
                down = [down[0] + trace_h[n - 2][0], down[1] + trace_h[n - 2][1]]
            current = [jj_ref[c, p] for c in range(3)] if 0 <= p < PLANES else None
            e[p] = next_electric(e[p], h[p], down, c_ref[0, p + 1], current, lanes)

    magnetic((-1, 7), 2)
    electric((0, 7, 8), 2)
    e[-1] = next_electric(e[-1], h[-1], (zero, zero), c_ref[0, 0], None, lanes)
    magnetic((-2, -1, 0, 6, 7, 8), 3)
    electric((-1, 0, 1, 6, 7, 8), 3)
    magnetic((-1, 0, 1, 5, 6, 7), 4)
    electric((0, 1, 2, 5, 6, 7), 4)
    for p in range(PLANES):
        for c in range(3):
            eo_ref[0, c, p] = e[p][c][:OWN]
            ho_ref[0, c, p] = h[p][c][:OWN]


def refine_weights():
    along_z = np.zeros((64, LANES), np.float32)
    for cell in range(LANES):
        along_z[cell // 2, cell] += 0.5
        along_z[min((cell + 1) // 2, 63), cell] += 0.5
    both = np.zeros((LANES, 2 * LANES), np.float32)
    both[:64, :LANES] = along_z
    both[64:, LANES:] = along_z
    along_y = np.zeros((ROWS, 16), np.float32)
    for row in range(ROWS):
        y = row if row < OWN + HALO else row - ROWS
        along_y[row, y // 2 + 2] += 0.5
        along_y[row, min((y + 1) // 2 + 2, 15)] += 0.5
    return both, along_y


def run(kernel, scalars, operands, outs, flops, scratch=(), steps=3, limit=60):
    def spec(shape, block):
        rank = len(shape)
        if block is pl.ANY:
            return pl.BlockSpec(memory_space=pl.ANY)
        if block is None:
            return pl.BlockSpec(tuple(shape), lambda r: (0,) * rank)
        if block is True:
            return pl.BlockSpec((1, *shape[1:]), lambda r: (r,) + (0,) * (rank - 1))
        block_shape, place = block
        return pl.BlockSpec(block_shape, lambda r: place)

    moved = sum(4 * int(np.prod(x.shape)) for x, _ in operands) + sum(4 * int(np.prod(x)) for x, _ in outs)
    return pl.pallas_call(
        kernel,
        grid=(steps,),
        in_specs=[pl.BlockSpec(memory_space=pltpu.SMEM)] * len(scalars)
        + [spec(x.shape, block) for x, block in operands],
        out_specs=[spec(shape, block) for shape, block in outs],
        out_shape=[jax.ShapeDtypeStruct(shape, jnp.float32) for shape, _ in outs],
        scratch_shapes=list(scratch),
        compiler_params=pltpu.CompilerParams(
            dimension_semantics=("arbitrary",), vmem_limit_bytes=limit * 1024 * 1024
        ),
        cost_estimate=pl.CostEstimate(flops=flops, bytes_accessed=moved, transcendentals=0),
        interpret=INTERPRET,
        name=kernel.__name__,
    )(*scalars, *[x for x, _ in operands])


def body(
    electric,
    magnetic,
    current,
    density_tiles,
    tile_slabs,
    design_box,
    material_mask,
    material_levels,
):
    wide_count = lax.axis_size("wide")
    wide_place = lax.axis_index("wide")
    narrow_count = lax.axis_size("narrow")
    narrow_place = lax.axis_index("narrow")
    core = wide_place % 2
    half = wide_count // 2

    near_pairs = [(w, w ^ 1) for w in range(wide_count)]
    partner = [(w + 1) % wide_count if w % 2 else (w - 1) % wide_count for w in range(wide_count)]
    far_ring = [(w, partner[w]) for w in range(wide_count)]
    far_pairs = [(w, partner[w]) for w in range(1, wide_count - 1)]
    up = [(n, n + 1) for n in range(narrow_count - 1)]
    down = [(n + 1, n) for n in range(narrow_count - 1)]
    groups = [[w for w in range(wide_count) if (w // 2) % 2 == side] for side in range(2)]

    mate = jnp.where(wide_place % 2 == 1, wide_place + 1, wide_place - 1 + wide_count) % wide_count
    slabs = jnp.stack([wide_place, mate])[:, None] + jnp.arange(-1, 2, dtype=jnp.int32)[None, :]
    slabs = jnp.clip(slabs, 0, wide_count - 1)
    ids = jnp.arange(wide_count, dtype=jnp.int32)
    at = jnp.sum(jnp.where(tile_slabs[None, None, :] == slabs[:, :, None], ids, 0), axis=2)
    here = ((at // 2) % 2 == (wide_place // 2) % 2).astype(jnp.int32)
    place = (at // 4) * 2 + at % 2
    table = jnp.concatenate(
        [
            jnp.stack([wide_place, narrow_place, core, jnp.int32(wide_count), jnp.int32(narrow_count)]),
            design_box,
            jnp.stack([place, here], axis=1).reshape(12),
        ]
    ).astype(jnp.int32)

    stack = [
        electric.reshape(72, OWN, LANES),
        magnetic.reshape(72, OWN, LANES),
        current.reshape(24, OWN, LANES),
        material_mask,
    ]
    ends = [(x, ((x.shape[0], 8, LANES), (0, row, 0))) for x in stack for row in (0, 2)]
    halo = (HALO_PLANES, HALO, LANES)
    first_rows, last_rows = run(pack_kernel, (), ends, [(halo, None), (halo, None)], 1_000_000, steps=1)
    tile = jnp.transpose(density_tiles, (1, 0, 2))
    tile_first, tile_last = run(
        tile_rows_kernel, (), [(tile, None)], [((4, LANES), None), ((4, LANES), None)], 1000, steps=1, limit=8
    )
    tile_lo = lax.ppermute(tile_last, "narrow", up)
    tile_hi = lax.ppermute(tile_first, "narrow", down)
    tile_lo, first_rows, last_rows = lax.optimization_barrier((tile_lo, first_rows, last_rows))
    low = lax.ppermute(last_rows, "narrow", up)
    high = lax.ppermute(first_rows, "narrow", down)
    (spread,) = run(
        tile_kernel,
        (table,),
        [(tile, None), (tile_lo, None), (tile_hi, None)],
        [((half, 4, 8, LANES), None)],
        1_000_000,
        steps=1,
        limit=8,
    )
    gathered = lax.all_to_all(spread, "wide", 0, 0, axis_index_groups=groups, tiled=True)
    gathered = gathered.reshape(half * 4, 8, LANES)

    extended = (3, 3, PLANES, ROWS, LANES)
    planes = (PLANES, ROWS, LANES)
    message = (3 * FIRST_TILES + 4, 8, LANES)
    e_ext, h_one, j_ext, m_ext, far, near = run(
        extend_kernel,
        (table,),
        [(electric, True), (magnetic, True), (current, None), (material_mask, None), (low, None), (high, None)],
        [(extended, True), (extended, True), ((3, *planes), None), (planes, None), (message, None), (message, None)],
        100_000_000_000,
    )
    near = lax.ppermute(near, "wide", near_pairs)

    mine, far = run(
        select_kernel,
        (table,),
        [(gathered, None), (far, pl.ANY)],
        [((COARSE, 8, LANES), None), ((COARSE + message[0], 8, LANES), None)],
        1_000_000,
        [pltpu.SemaphoreType.DMA],
        steps=1,
        limit=8,
    )
    far = lax.ppermute(far, "wide", far_ring)
    fields = [(e_ext, True), (h_one, True), (j_ext, None)]

    weights_z, weights_y = refine_weights()
    message = (3 * TILES, 8, LANES)
    coefficients = (3, PLANES + 2, ROWS, LANES)
    strips = pltpu.VMEM((COARSE, ROWS, LANES), jnp.float32)
    still = (e_ext, h_one, j_ext, m_ext, weights_z, weights_y)
    e_on, h_on, j_on, m_on, z_on, y_on = run(
        stage_kernel,
        (),
        [(x, i < 2 or None) for i, x in enumerate(still)],
        [(x.shape, i < 2 or None) for i, x in enumerate(still)],
        1_000_000_000,
        limit=10,
    )
    far_end, near_end = run(
        trace_kernel,
        (table, material_levels),
        [(x, None) for x in (mine, z_on, y_on, m_on, far, near)] + [(e_on, None), (h_on, None), (j_on, None)],
        [(message, None), (message, None)],
        10_000_000,
        [pltpu.VMEM(coefficients, jnp.float32), strips],
        steps=1,
        limit=24,
    )
    inputs = [(x, None) for x in (mine, weights_z, weights_y, m_ext, far, near)] + fields
    near_end = lax.ppermute(near_end, "wide", near_pairs)
    far_end = lax.ppermute(far_end, "wide", far_pairs)

    e_in, h_in, coefficient = run(
        inner_kernel,
        (table, material_levels),
        inputs,
        [(extended, True), (extended, True), (coefficients, None)],
        10_000_000,
        [strips],
        limit=24,
    )
    own = (3, 3, PLANES, OWN, LANES)
    return tuple(
        run(
            window_kernel,
            (table,),
            [(coefficient, True), (far_end, None), (near_end, None), (e_in, True), (h_in, True), (j_ext, None)],
            [(own, True), (own, True)],
            10_000_000,
            limit=24,
        )
    )


def solution(mesh):
    return jax.shard_map(
        body,
        mesh=mesh,
        in_specs=(
            P(None, None, "wide", "narrow", None),
            P(None, None, "wide", "narrow", None),
            P(None, "wide", "narrow", None),
            P("wide", "narrow", None),
            P(),
            P(),
            P("wide", "narrow", None),
            P(),
        ),
        out_specs=(P(None, None, "wide", "narrow", None), P(None, None, "wide", "narrow", None)),
        check_vma=False,
    )
```

```python
import jax
import jax.numpy as jnp
import numpy as np
from jax import lax
from jax.experimental import pallas as pl
from jax.experimental.pallas import tpu as pltpu
from jax.sharding import PartitionSpec as P

STEPS = 4
PLANES = 8
OWN = 24
ROWS = 32
HALO = 4
LANES = 128
FIRST_TILES = 8
COARSE = 6
TILES = 21

sharpness = 8.0
thresholds = (0.7, 0.5, 0.3)
time_step = 0.5

INTERPRET = False


def lane_ids():
    return lax.broadcasted_iota(jnp.int32, (ROWS, LANES), 1)


def row_ids():
    rows = lax.broadcasted_iota(jnp.int32, (ROWS, LANES), 0)
    return jnp.where(rows < OWN + HALO, rows, rows - ROWS)


def y_forward(a):
    return pltpu.roll(a, ROWS - 1, 0) - a


def y_backward(a):
    return a - pltpu.roll(a, 1, 0)


def z_forward(a, lanes):
    return jnp.where(lanes == LANES - 1, 0.0, pltpu.roll(a, LANES - 1, 1)) - a


def z_backward(a, lanes):
    return a - jnp.where(lanes == 0, 0.0, pltpu.roll(a, 1, 1))


def next_magnetic(h, e, e_up, step, lanes):
    up_y, up_z = e_up
    curl_x = y_forward(e[2]) - z_forward(e[1], lanes)
    curl_y = z_forward(e[0], lanes) - (up_z - e[2])
    curl_z = (up_y - e[1]) - y_forward(e[0])
    return [h[0] - step * curl_x, h[1] - step * curl_y, h[2] - step * curl_z]


def next_electric(e, h, h_down, coefficient, current, lanes):
    down_y, down_z = h_down
    curls = [
        y_backward(h[2]) - z_backward(h[1], lanes),
        z_backward(h[0], lanes) - (h[2] - down_z),
        (h[1] - down_y) - y_backward(h[0]),
    ]
    if current is not None:
        curls = [curls[c] - current[c] for c in range(3)]
    return [e[c] + coefficient * curls[c] for c in range(3)]


def step_of_rows(narrow_place):
    return jnp.where((row_ids() < 0) & (narrow_place == 0), 0.0, time_step)


WIDE, NARROW, CORE, WIDE_COUNT, NARROW_COUNT, BOX, MINE, THEIRS = 0, 1, 2, 3, 4, 5, 11, 17
E_AT, H_AT, J_AT, MASK_AT, HALO_PLANES = 0, 72, 144, 168, 176


def tiles_of(plane, count=4):
    return [plane[8 * i : 8 * i + 8] for i in range(count)]


def select(condition, yes, no):
    return [jnp.where(condition, a, b) for a, b in zip(yes, no, strict=True)]


def pack_kernel(
    e_first, e_last, h_first, h_last, j_first, j_last, m_first, m_last, tile_ref,
    first_ref, last_ref, tile_first, tile_last,
):
    tile_first[...] = jnp.concatenate([tile_ref[0], tile_ref[1]], axis=1)
    tile_last[...] = jnp.concatenate([tile_ref[10], tile_ref[11]], axis=1)
    for at, count, first, last in (
        (E_AT, 72, e_first, e_last),
        (H_AT, 72, h_first, h_last),
        (J_AT, 24, j_first, j_last),
        (MASK_AT, PLANES, m_first, m_last),
    ):
        first_ref[at : at + count] = first[:, :HALO].astype(jnp.float32)
        last_ref[at : at + count] = last[:, 8 - HALO :].astype(jnp.float32)


def tile_kernel(table, tile_ref, lo_ref, hi_ref, spread_ref):
    top = table[NARROW] == table[NARROW_COUNT] - 1
    for q in range(4):
        tile = jnp.concatenate([tile_ref[row, q : q + 1] for row in range(12)], axis=0)
        lo, hi = lo_ref[q : q + 1], hi_ref[q : q + 1]
        above = jnp.concatenate([hi[:, :64], hi[:, 64:]], axis=0)
        above = jnp.where(top, jnp.broadcast_to(tile[11:12], (2, 64)), above)
        first = jnp.concatenate([lo[:, :64], lo[:, 64:], tile[:6]], axis=0)
        second = jnp.concatenate([tile[6:], above], axis=0)
        packed = jnp.concatenate([first, second], axis=1)
        for i in range(spread_ref.shape[0]):
            spread_ref[i, q] = packed


def select_kernel(table, g_ref, message_ref, mine_ref, far_ref, sem):
    copy = pltpu.make_async_copy(message_ref, far_ref.at[pl.ds(COARSE, 3 * FIRST_TILES + 4)], sem)
    copy.start()
    for at, ref in ((MINE, mine_ref), (THEIRS, far_ref)):
        for i, (which, q) in enumerate(((0, 3), (1, 0), (1, 1), (1, 2), (1, 3), (2, 0))):
            held = g_ref[table[at + which] * 4 + q]
            ref[i] = jnp.where(table[at + 3 + which] == 1, held, 0.0)
    copy.wait()


def extend_kernel(
    table, e_ref, h_ref, j_ref, m_ref, lo_ref, hi_ref, ee_ref, h1_ref, jj_ref, mm_ref, far_ref, near_ref
):
    r = pl.program_id(0)
    lanes = lane_ids()
    step = step_of_rows(table[NARROW])
    core = table[CORE]
    zero = jnp.zeros((ROWS, LANES), jnp.float32)

    def extended(own, at):
        return jnp.concatenate([own, hi_ref[at], lo_ref[at]], axis=0)

    up = [zero] * 3
    upward = downward = None
    for p in range(PLANES - 1, -1, -1):
        at = r * 24 + p
        e = [extended(e_ref[0, c, p], E_AT + at + c * PLANES) for c in range(3)]
        h = [extended(h_ref[0, c, p], H_AT + at + c * PLANES) for c in range(3)]
        new = next_magnetic(h, e, (up[1], up[2]), step, lanes)
        for c in range(3):
            ee_ref[0, c, p] = e[c]
            h1_ref[0, c, p] = new[c]
        if p == PLANES - 1:
            upward = tiles_of(new[1]) + tiles_of(new[2])
        if p == 0:
            downward = tiles_of(e[1]) + tiles_of(e[2])
        up = e
    far, near = select(core == 1, upward, downward), select(core == 1, downward, upward)
    for i in range(FIRST_TILES):
        far_ref[r * FIRST_TILES + i] = far[i]
        near_ref[r * FIRST_TILES + i] = near[i]

    @pl.when(r == 0)
    def _():
        for p in range(PLANES):
            for c in range(3):
                jj_ref[c, p] = extended(j_ref[c, p], J_AT + c * PLANES + p)
            mm_ref[p] = extended(m_ref[p].astype(jnp.float32), MASK_AT + p)
        above, below = tiles_of(mm_ref[PLANES - 1]), tiles_of(mm_ref[0])
        far, near = select(core == 1, above, below), select(core == 1, below, above)
        for i in range(4):
            far_ref[3 * FIRST_TILES + i] = far[i]
            near_ref[3 * FIRST_TILES + i] = near[i]


def coefficients_of(density, mask, global_x, table, levels, lanes):
    m0, m1 = levels[0], levels[1]
    global_y = table[NARROW] * OWN + row_ids()
    inside = (
        (global_x >= table[BOX])
        & (global_x < table[BOX + 1])
        & (global_y >= table[BOX + 2])
        & (global_y < table[BOX + 3])
        & (lanes >= table[BOX + 4])
        & (lanes < table[BOX + 5])
    )
    in_grid = (
        (global_x >= 0)
        & (global_x < table[WIDE_COUNT] * PLANES)
        & (global_y >= 0)
        & (global_y < table[NARROW_COUNT] * OWN)
    )
    background = jnp.where(mask > 0.5, m1, m0)
    out = []
    for threshold in thresholds:
        base = float(np.tanh(sharpness * threshold))
        scale = 1.0 / (base + float(np.tanh(sharpness * (1.0 - threshold))))
        projected = (base + jnp.tanh(sharpness * (density - threshold))) * scale
        permittivity = jnp.where(inside, m0 + projected * (m1 - m0), background)
        out.append(jnp.where(in_grid, time_step / permittivity, 0.0))
    return out


def first_message(ref, at):
    return [jnp.concatenate([ref[at + 4 * c + i] for i in range(4)], axis=0) for c in range(2)]


def first_state(r, block, table, ee_ref, h1_ref, far_ref, near_ref, step):
    core = table[CORE]
    far, near = first_message(far_ref, COARSE + r * FIRST_TILES), first_message(near_ref, r * FIRST_TILES)
    trace_h = [jnp.where(table[WIDE] == 0, 0.0, x) for x in select(core == 0, far, near)]
    trace_e = [jnp.where(table[WIDE] == table[WIDE_COUNT] - 1, 0.0, x) for x in select(core == 1, far, near)]
    e = {p: [ee_ref[block, c, p] for c in range(3)] for p in range(PLANES)}
    h = {p: [h1_ref[block, c, p] for c in range(3)] for p in range(PLANES)}
    top = PLANES - 1
    h[top] = [h[top][0], h[top][1] + step * trace_e[1], h[top][2] - step * trace_e[0]]
    below = jnp.where(table[WIDE] == 0, 0.0, step)
    h[-1] = [None, trace_h[0] + below * e[0][2], trace_h[1] - below * e[0][1]]
    return e, h


def as_message(traces):
    rows = lax.broadcasted_iota(jnp.int32, (8, LANES), 0)
    tiles = []
    for n in range(3):
        for c in range(2):
            tiles += tiles_of(traces[n][c], 3)
    halo = [[traces[n][c][OWN:] for c in range(2)] for n in range(3)]
    for c in range(2):
        tiles.append(jnp.where((rows > 1) & (rows < 5), pltpu.roll(halo[1][c], 4, 0), halo[0][c]))
    tiles.append(jnp.where(rows == 3, pltpu.roll(halo[2][1], 4, 0), halo[2][0]))
    return tiles


def from_message(tile):
    traces = []
    for n in range(3):
        step = []
        for c in range(2):
            halo = tile(20) if n == 2 else tile(18 + c)
            halo = pltpu.roll(halo, 4, 0) if n == 1 or (n == 2 and c == 1) else halo
            step.append(jnp.concatenate([tile((n * 2 + c) * 3 + i) for i in range(3)] + [halo], axis=0))
        traces.append(step)
    return traces


def refine(table, mine_ref, far_ref, wz_ref, wy_ref, d_ref):
    last = table[WIDE] == table[WIDE_COUNT] - 1
    coarse = [mine_ref[q] + far_ref[q] for q in range(COARSE)]
    coarse[5] = jnp.where(last, coarse[4], coarse[5])
    along_z = jnp.dot(
        jnp.concatenate(coarse, axis=0),
        wz_ref[...],
        precision=lax.Precision.HIGHEST,
        preferred_element_type=jnp.float32,
    )
    strips = [
        jnp.concatenate([along_z[8 * q : 8 * q + 8, :LANES], along_z[8 * q : 8 * q + 8, LANES:]], axis=0)
        for q in range(COARSE)
    ]
    along_y = jnp.dot(
        wy_ref[...],
        jnp.concatenate(strips, axis=1),
        precision=lax.Precision.HIGHEST,
        preferred_element_type=jnp.float32,
    )
    for q in range(COARSE):
        d_ref[q] = along_y[:, LANES * q : LANES * (q + 1)]


def plane_coefficients(p, mask, table, levels, d_ref, c_ref):
    q = 1 + p // 2
    density = d_ref[q] if p % 2 == 0 else 0.5 * (d_ref[q] + d_ref[q + 1])
    values = coefficients_of(density, mask, table[WIDE] * PLANES + p, table, levels, lane_ids())
    for r in range(3):
        c_ref[r, p + 1] = values[r]


def trace_kernel(
    table, levels, mine_ref, wz_ref, wy_ref, mm_ref, far_ref, near_ref, ee_ref, h1_ref, jj_ref,
    far_out, near_out, c_ref, d_ref,
):
    refine(table, mine_ref, far_ref, wz_ref, wy_ref, d_ref)
    for p in (0, 1, 2, 5, 6, 7):
        plane_coefficients(p, mm_ref[p], table, levels, d_ref, c_ref)
    lanes = lane_ids()
    step = step_of_rows(table[NARROW])
    core = table[CORE]
    zero = jnp.zeros((ROWS, LANES), jnp.float32)

    def per_real(r, carry):
        e, h = first_state(r, r, table, ee_ref, h1_ref, far_ref, near_ref, step)

        def electric(p):
            current = [jj_ref[c, p] for c in range(3)]
            e[p] = next_electric(e[p], h[p], (h[p - 1][1], h[p - 1][2]), c_ref[r, p + 1], current, lanes)

        def magnetic(p):
            h[p] = next_magnetic(h[p], e[p], (e[p + 1][1], e[p + 1][2]), step, lanes)

        for p in (0, 1, 2, 5, 6, 7):
            electric(p)
        h[-1] = [zero] * 3
        e[8] = [zero] * 3
        upward, downward = [], [(e[0][1], e[0][2])]
        for first in (5, 6, 7):
            for p in range(first, 8):
                magnetic(p)
            upward.append((h[7][1], h[7][2]))
            for p in range(first + 1, 8):
                electric(p)
        for last_plane in (1, 0):
            for p in range(last_plane + 1):
                magnetic(p)
            for p in range(last_plane + 1):
                electric(p)
            downward.append((e[0][1], e[0][2]))
        for i, (a, b) in enumerate(zip(as_message(upward), as_message(downward), strict=True)):
            far_out[r * TILES + i] = jnp.where(core == 1, a, b)
            near_out[r * TILES + i] = jnp.where(core == 1, b, a)
        return carry

    lax.fori_loop(0, 3, per_real, 0)


def stage_kernel(*refs):
    for source, copied in zip(refs[: len(refs) // 2], refs[len(refs) // 2 :], strict=True):
        copied[...] = source[...]


def inner_kernel(
    table, levels, mine_ref, wz_ref, wy_ref, mm_ref, far_ref, near_ref, ee_ref, h1_ref, jj_ref,
    eo_ref, ho_ref, c_ref, d_ref,
):
    r = pl.program_id(0)

    @pl.when(r == 0)
    def _():
        refine(table, mine_ref, far_ref, wz_ref, wy_ref, d_ref)
        core = table[CORE]
        far = jnp.concatenate([far_ref[COARSE + 3 * FIRST_TILES + i] for i in range(4)], axis=0)
        near = jnp.concatenate([near_ref[3 * FIRST_TILES + i] for i in range(4)], axis=0)
        for p in range(-1, PLANES + 1):
            if p < 0:
                mask = jnp.where(core == 0, far, near)
            else:
                mask = mm_ref[p] if p < PLANES else jnp.where(core == 1, far, near)
            plane_coefficients(p, mask, table, levels, d_ref, c_ref)

    lanes = lane_ids()
    step = step_of_rows(table[NARROW])
    e, h = first_state(r, 0, table, ee_ref, h1_ref, far_ref, near_ref, step)

    def electric(first, last):
        for p in range(first, last + 1):
            current = [jj_ref[c, p] for c in range(3)]
            e[p] = next_electric(e[p], h[p], (h[p - 1][1], h[p - 1][2]), c_ref[r, p + 1], current, lanes)

    def magnetic(first, last):
        for p in range(first, last + 1):
            h[p] = next_magnetic(h[p], e[p], (e[p + 1][1], e[p + 1][2]), step, lanes)

    electric(0, 7)
    magnetic(0, 6)
    electric(1, 6)
    magnetic(1, 5)
    electric(2, 5)
    magnetic(2, 4)
    electric(3, 4)
    for p in range(PLANES):
        for c in range(3):
            eo_ref[0, c, p] = e[p][c]
            ho_ref[0, c, p] = h[p][c]


def window_kernel(table, c_ref, far_ref, near_ref, ee_ref, hh_ref, jj_ref, eo_hbm, ho_hbm, eo_ref, ho_ref, sems):
    lanes = lane_ids()
    core = table[CORE]
    step = step_of_rows(table[NARROW])
    below = jnp.where(table[WIDE] == 0, 0.0, step)
    zero = jnp.zeros((ROWS, LANES), jnp.float32)

    def written(r):
        return [
            pltpu.make_async_copy(eo_ref.at[r], eo_hbm.at[r], sems.at[0, r]),
            pltpu.make_async_copy(ho_ref.at[r], ho_hbm.at[r], sems.at[1, r]),
        ]

    def per_real(r, carry):
        def tile_from_below(i):
            return jnp.where(core == 0, far_ref[r * TILES + i], near_ref[r * TILES + i])

        def tile_from_above(i):
            return jnp.where(core == 1, far_ref[r * TILES + i], near_ref[r * TILES + i])

        trace_h = from_message(tile_from_below)
        trace_e = from_message(tile_from_above)
        e = {p: [zero] * 3 for p in (-2, -1, 8, 9)}
        h = {p: [zero] * 3 for p in (-2, -1, 8)}
        for p in range(PLANES):
            e[p] = [ee_ref[r, c, p] for c in range(3)]
            h[p] = [hh_ref[r, c, p] for c in range(3)]

        def magnetic(planes, n):
            for p in planes:
                up = [e[p + 1][1], e[p + 1][2]]
                if p == 7:
                    up = [up[0] + trace_e[n - 2][0], up[1] + trace_e[n - 2][1]]
                h[p] = next_magnetic(h[p], e[p], up, below if p < 0 else step, lanes)

        def electric(planes, n):
            for p in planes:
                down = [h[p - 1][1], h[p - 1][2]]
                if p == 0:
                    down = [down[0] + trace_h[n - 2][0], down[1] + trace_h[n - 2][1]]
                current = [jj_ref[c, p] for c in range(3)] if 0 <= p < PLANES else None
                e[p] = next_electric(e[p], h[p], down, c_ref[r, p + 1], current, lanes)

        magnetic((-1, 7), 2)
        electric((0, 7, 8), 2)
        e[-1] = next_electric(e[-1], h[-1], (zero, zero), c_ref[r, 0], None, lanes)
        magnetic((-2, -1, 0, 6, 7, 8), 3)
        electric((-1, 0, 1, 6, 7, 8), 3)
        magnetic((-1, 0, 1, 5, 6, 7), 4)
        electric((0, 1, 2, 5, 6, 7), 4)
        for p in range(PLANES):
            for c in range(3):
                eo_ref[r, c, p] = e[p][c][:OWN]
                ho_ref[r, c, p] = h[p][c][:OWN]
        for copy in written(r):
            copy.start()
        return carry

    lax.fori_loop(0, 3, per_real, 0)
    for r in range(3):
        for copy in written(r):
            copy.wait()


def refine_weights():
    along_z = np.zeros((64, LANES), np.float32)
    for cell in range(LANES):
        along_z[cell // 2, cell] += 0.5
        along_z[min((cell + 1) // 2, 63), cell] += 0.5
    both = np.zeros((LANES, 2 * LANES), np.float32)
    both[:64, :LANES] = along_z
    both[64:, LANES:] = along_z
    along_y = np.zeros((ROWS, 16), np.float32)
    for row in range(ROWS):
        y = row if row < OWN + HALO else row - ROWS
        along_y[row, y // 2 + 2] += 0.5
        along_y[row, min((y + 1) // 2 + 2, 15)] += 0.5
    return both, along_y


def run(kernel, scalars, operands, outs, flops, scratch=(), steps=3, limit=60):
    def spec(shape, block):
        rank = len(shape)
        if block is pl.ANY:
            return pl.BlockSpec(memory_space=pl.ANY)
        if block is None:
            return pl.BlockSpec(tuple(shape), lambda r: (0,) * rank)
        if block is True:
            return pl.BlockSpec((1, *shape[1:]), lambda r: (r,) + (0,) * (rank - 1))
        block_shape, place = block
        return pl.BlockSpec(block_shape, lambda r: place)

    moved = sum(4 * int(np.prod(x.shape)) for x, _ in operands) + sum(4 * int(np.prod(x)) for x, _ in outs)
    return pl.pallas_call(
        kernel,
        grid=(steps,),
        in_specs=[pl.BlockSpec(memory_space=pltpu.SMEM)] * len(scalars)
        + [spec(x.shape, block) for x, block in operands],
        out_specs=[spec(shape, block) for shape, block in outs],
        out_shape=[jax.ShapeDtypeStruct(shape, jnp.float32) for shape, _ in outs],
        scratch_shapes=list(scratch),
        compiler_params=pltpu.CompilerParams(
            dimension_semantics=("arbitrary",), vmem_limit_bytes=limit * 1024 * 1024
        ),
        cost_estimate=pl.CostEstimate(flops=flops, bytes_accessed=moved, transcendentals=0),
        interpret=INTERPRET,
        name=kernel.__name__,
    )(*scalars, *[x for x, _ in operands])


def run_in_place(kernel, scalars, operands, outs, scratch, out_space, limit):
    return pl.pallas_call(
        kernel,
        in_specs=[pl.BlockSpec(memory_space=pltpu.SMEM)] * len(scalars)
        + [pl.BlockSpec(memory_space=pltpu.VMEM)] * len(operands),
        out_specs=[pl.BlockSpec(memory_space=out_space)] * len(outs),
        out_shape=[jax.ShapeDtypeStruct(shape, jnp.float32) for shape in outs],
        scratch_shapes=list(scratch),
        compiler_params=pltpu.CompilerParams(vmem_limit_bytes=limit * 1024 * 1024),
        cost_estimate=pl.CostEstimate(flops=10_000_000, bytes_accessed=10_000_000, transcendentals=0),
        interpret=INTERPRET,
        name=kernel.__name__,
    )(*scalars, *operands)


def body(
    electric,
    magnetic,
    current,
    density_tiles,
    tile_slabs,
    design_box,
    material_mask,
    material_levels,
):
    wide_count = lax.axis_size("wide")
    wide_place = lax.axis_index("wide")
    narrow_count = lax.axis_size("narrow")
    narrow_place = lax.axis_index("narrow")
    core = wide_place % 2
    half = wide_count // 2

    near_pairs = [(w, w ^ 1) for w in range(wide_count)]
    partner = [(w + 1) % wide_count if w % 2 else (w - 1) % wide_count for w in range(wide_count)]
    far_ring = [(w, partner[w]) for w in range(wide_count)]
    far_pairs = [(w, partner[w]) for w in range(1, wide_count - 1)]
    up = [(n, n + 1) for n in range(narrow_count - 1)]
    down = [(n + 1, n) for n in range(narrow_count - 1)]
    groups = [[w for w in range(wide_count) if (w // 2) % 2 == side] for side in range(2)]

    mate = jnp.where(wide_place % 2 == 1, wide_place + 1, wide_place - 1 + wide_count) % wide_count
    slabs = jnp.stack([wide_place, mate])[:, None] + jnp.arange(-1, 2, dtype=jnp.int32)[None, :]
    slabs = jnp.clip(slabs, 0, wide_count - 1)
    ids = jnp.arange(wide_count, dtype=jnp.int32)
    at = jnp.sum(jnp.where(tile_slabs[None, None, :] == slabs[:, :, None], ids, 0), axis=2)
    here = ((at // 2) % 2 == (wide_place // 2) % 2).astype(jnp.int32)
    place = (at // 4) * 2 + at % 2
    table = jnp.concatenate(
        [
            jnp.stack([wide_place, narrow_place, core, jnp.int32(wide_count), jnp.int32(narrow_count)]),
            design_box,
            jnp.stack([place, here], axis=1).reshape(12),
        ]
    ).astype(jnp.int32)

    stack = [
        electric.reshape(72, OWN, LANES),
        magnetic.reshape(72, OWN, LANES),
        current.reshape(24, OWN, LANES),
        material_mask,
    ]
    ends = [(x, ((x.shape[0], 8, LANES), (0, row, 0))) for x in stack for row in (0, 2)]
    halo = (HALO_PLANES, HALO, LANES)
    tile = jnp.transpose(density_tiles, (1, 0, 2))
    first_rows, last_rows, tile_first, tile_last = run(
        pack_kernel,
        (),
        ends + [(tile, None)],
        [(halo, None), (halo, None), ((4, LANES), None), ((4, LANES), None)],
        1_000_000,
        steps=1,
    )
    tile_lo = lax.ppermute(tile_last, "narrow", up)
    tile_hi = lax.ppermute(tile_first, "narrow", down)
    tile_lo, first_rows, last_rows = lax.optimization_barrier((tile_lo, first_rows, last_rows))
    low = lax.ppermute(last_rows, "narrow", up)
    high = lax.ppermute(first_rows, "narrow", down)
    (spread,) = run(
        tile_kernel,
        (table,),
        [(tile, None), (tile_lo, None), (tile_hi, None)],
        [((half, 4, 8, LANES), None)],
        1_000_000,
        steps=1,
        limit=8,
    )
    gathered = lax.all_to_all(spread, "wide", 0, 0, axis_index_groups=groups, tiled=True)
    gathered = gathered.reshape(half * 4, 8, LANES)

    extended = (3, 3, PLANES, ROWS, LANES)
    planes = (PLANES, ROWS, LANES)
    message = (3 * FIRST_TILES + 4, 8, LANES)
    e_ext, h_one, j_ext, m_ext, far, near = run(
        extend_kernel,
        (table,),
        [(electric, True), (magnetic, True), (current, None), (material_mask, None), (low, None), (high, None)],
        [(extended, True), (extended, True), ((3, *planes), None), (planes, None), (message, None), (message, None)],
        100_000_000_000,
    )
    near = lax.ppermute(near, "wide", near_pairs)

    mine, far = run(
        select_kernel,
        (table,),
        [(gathered, None), (far, pl.ANY)],
        [((COARSE, 8, LANES), None), ((COARSE + message[0], 8, LANES), None)],
        1_000_000,
        [pltpu.SemaphoreType.DMA],
        steps=1,
        limit=8,
    )
    far = lax.ppermute(far, "wide", far_ring)
    fields = [(e_ext, True), (h_one, True), (j_ext, None)]

    weights_z, weights_y = refine_weights()
    message = (3 * TILES, 8, LANES)
    coefficients = (3, PLANES + 2, ROWS, LANES)
    strips = pltpu.VMEM((COARSE, ROWS, LANES), jnp.float32)
    still = (e_ext, h_one, j_ext, m_ext, weights_z, weights_y)
    e_on, h_on, j_on, m_on, z_on, y_on = run(
        stage_kernel,
        (),
        [(x, i < 2 or None) for i, x in enumerate(still)],
        [(x.shape, i < 2 or None) for i, x in enumerate(still)],
        1_000_000_000,
        limit=10,
    )
    far_end, near_end = run_in_place(
        trace_kernel,
        (table, material_levels),
        (mine, z_on, y_on, m_on, far, near, e_on, h_on, j_on),
        [message, message],
        [pltpu.VMEM(coefficients, jnp.float32), strips],
        pltpu.VMEM,
        16,
    )
    inputs = [(x, None) for x in (mine, weights_z, weights_y, m_ext, far, near)] + fields
    near_end = lax.ppermute(near_end, "wide", near_pairs)
    far_end = lax.ppermute(far_end, "wide", far_pairs)

    e_in, h_in, coefficient = run(
        inner_kernel,
        (table, material_levels),
        inputs,
        [(extended, True), (extended, True), (coefficients, None)],
        10_000_000,
        [strips],
        limit=24,
    )
    own = (3, 3, PLANES, OWN, LANES)
    return tuple(
        run_in_place(
            window_kernel,
            (table,),
            (coefficient, far_end, near_end, e_in, h_in, j_ext),
            [own, own],
            [pltpu.VMEM(own, jnp.float32), pltpu.VMEM(own, jnp.float32), pltpu.SemaphoreType.DMA((2, 3))],
            pltpu.HBM,
            16,
        )
    )


def solution(mesh):
    return jax.shard_map(
        body,
        mesh=mesh,
        in_specs=(
            P(None, None, "wide", "narrow", None),
            P(None, None, "wide", "narrow", None),
            P(None, "wide", "narrow", None),
            P("wide", "narrow", None),
            P(),
            P(),
            P("wide", "narrow", None),
            P(),
        ),
        out_specs=(P(None, None, "wide", "narrow", None), P(None, None, "wide", "narrow", None)),
        check_vma=False,
    )
```

```python
import jax
import jax.numpy as jnp
import numpy as np
from jax import lax
from jax.experimental import pallas as pl
from jax.experimental.pallas import tpu as pltpu
from jax.sharding import PartitionSpec as P

STEPS = 4
PLANES = 8
OWN = 24
ROWS = 32
HALO = 4
LANES = 128
FIRST_TILES = 8
COARSE = 6
TILES = 21

sharpness = 8.0
thresholds = (0.7, 0.5, 0.3)
time_step = 0.5

INTERPRET = False


def lane_ids():
    return lax.broadcasted_iota(jnp.int32, (ROWS, LANES), 1)


def row_ids():
    rows = lax.broadcasted_iota(jnp.int32, (ROWS, LANES), 0)
    return jnp.where(rows < OWN + HALO, rows, rows - ROWS)


def y_forward(a):
    return pltpu.roll(a, ROWS - 1, 0) - a


def y_backward(a):
    return a - pltpu.roll(a, 1, 0)


def z_forward(a, lanes):
    return jnp.where(lanes == LANES - 1, 0.0, pltpu.roll(a, LANES - 1, 1)) - a


def z_backward(a, lanes):
    return a - jnp.where(lanes == 0, 0.0, pltpu.roll(a, 1, 1))


def next_magnetic(h, e, e_up, step, lanes):
    up_y, up_z = e_up
    curl_x = y_forward(e[2]) - z_forward(e[1], lanes)
    curl_y = z_forward(e[0], lanes) - (up_z - e[2])
    curl_z = (up_y - e[1]) - y_forward(e[0])
    return [h[0] - step * curl_x, h[1] - step * curl_y, h[2] - step * curl_z]


def next_electric(e, h, h_down, coefficient, current, lanes):
    down_y, down_z = h_down
    curls = [
        y_backward(h[2]) - z_backward(h[1], lanes),
        z_backward(h[0], lanes) - (h[2] - down_z),
        (h[1] - down_y) - y_backward(h[0]),
    ]
    if current is not None:
        curls = [curls[c] - current[c] for c in range(3)]
    return [e[c] + coefficient * curls[c] for c in range(3)]


def step_of_rows(narrow_place):
    return jnp.where((row_ids() < 0) & (narrow_place == 0), 0.0, time_step)


WIDE, NARROW, CORE, WIDE_COUNT, NARROW_COUNT, BOX, MINE, THEIRS = 0, 1, 2, 3, 4, 5, 11, 17
E_AT, H_AT, J_AT, MASK_AT, HALO_PLANES = 0, 72, 144, 168, 176


def tiles_of(plane, count=4):
    return [plane[8 * i : 8 * i + 8] for i in range(count)]


def select(condition, yes, no):
    return [jnp.where(condition, a, b) for a, b in zip(yes, no, strict=True)]


def pack_kernel(
    e_first, e_last, h_first, h_last, j_first, j_last, m_first, m_last, tile_ref,
    first_ref, last_ref, tile_first, tile_last,
):
    tile_first[...] = jnp.concatenate([tile_ref[0], tile_ref[1]], axis=1)
    tile_last[...] = jnp.concatenate([tile_ref[10], tile_ref[11]], axis=1)
    for at, count, first, last in (
        (E_AT, 72, e_first, e_last),
        (H_AT, 72, h_first, h_last),
        (J_AT, 24, j_first, j_last),
        (MASK_AT, PLANES, m_first, m_last),
    ):
        first_ref[at : at + count] = first[:, :HALO].astype(jnp.float32)
        last_ref[at : at + count] = last[:, 8 - HALO :].astype(jnp.float32)


def tile_kernel(table, tile_ref, lo_ref, hi_ref, spread_ref):
    top = table[NARROW] == table[NARROW_COUNT] - 1
    for q in range(4):
        tile = jnp.concatenate([tile_ref[row, q : q + 1] for row in range(12)], axis=0)
        lo, hi = lo_ref[q : q + 1], hi_ref[q : q + 1]
        above = jnp.concatenate([hi[:, :64], hi[:, 64:]], axis=0)
        above = jnp.where(top, jnp.broadcast_to(tile[11:12], (2, 64)), above)
        first = jnp.concatenate([lo[:, :64], lo[:, 64:], tile[:6]], axis=0)
        second = jnp.concatenate([tile[6:], above], axis=0)
        packed = jnp.concatenate([first, second], axis=1)
        for i in range(spread_ref.shape[0]):
            spread_ref[i, q] = packed


def select_kernel(table, g_ref, mine_ref, theirs_ref):
    for at, ref in ((MINE, mine_ref), (THEIRS, theirs_ref)):
        for i, (which, q) in enumerate(((0, 3), (1, 0), (1, 1), (1, 2), (1, 3), (2, 0))):
            held = g_ref[table[at + which] * 4 + q]
            ref[i] = jnp.where(table[at + 3 + which] == 1, held, 0.0)


def extend_kernel(
    table, e_ref, h_ref, j_ref, m_ref, lo_ref, hi_ref, ee_ref, h1_ref, jj_ref, mm_ref, far_ref, near_ref
):
    r = pl.program_id(0)
    lanes = lane_ids()
    step = step_of_rows(table[NARROW])
    core = table[CORE]
    zero = jnp.zeros((ROWS, LANES), jnp.float32)

    def extended(own, at):
        return jnp.concatenate([own, hi_ref[at], lo_ref[at]], axis=0)

    up = [zero] * 3
    upward = downward = None
    for p in range(PLANES - 1, -1, -1):
        at = r * 24 + p
        e = [extended(e_ref[0, c, p], E_AT + at + c * PLANES) for c in range(3)]
        h = [extended(h_ref[0, c, p], H_AT + at + c * PLANES) for c in range(3)]
        new = next_magnetic(h, e, (up[1], up[2]), step, lanes)
        for c in range(3):
            ee_ref[0, c, p] = e[c]
            h1_ref[0, c, p] = new[c]
        if p == PLANES - 1:
            upward = tiles_of(new[1]) + tiles_of(new[2])
        if p == 0:
            downward = tiles_of(e[1]) + tiles_of(e[2])
        up = e
    far, near = select(core == 1, upward, downward), select(core == 1, downward, upward)
    for i in range(FIRST_TILES):
        far_ref[COARSE + r * FIRST_TILES + i] = far[i]
        near_ref[r * FIRST_TILES + i] = near[i]

    @pl.when(r == 0)
    def _():
        for p in range(PLANES):
            for c in range(3):
                jj_ref[c, p] = extended(j_ref[c, p], J_AT + c * PLANES + p)
            mm_ref[p] = extended(m_ref[p].astype(jnp.float32), MASK_AT + p)
        above, below = tiles_of(mm_ref[PLANES - 1]), tiles_of(mm_ref[0])
        far, near = select(core == 1, above, below), select(core == 1, below, above)
        for i in range(4):
            far_ref[COARSE + 3 * FIRST_TILES + i] = far[i]
            near_ref[3 * FIRST_TILES + i] = near[i]


def coefficients_of(density, mask, global_x, table, levels, lanes):
    m0, m1 = levels[0], levels[1]
    global_y = table[NARROW] * OWN + row_ids()
    inside = (
        (global_x >= table[BOX])
        & (global_x < table[BOX + 1])
        & (global_y >= table[BOX + 2])
        & (global_y < table[BOX + 3])
        & (lanes >= table[BOX + 4])
        & (lanes < table[BOX + 5])
    )
    in_grid = (
        (global_x >= 0)
        & (global_x < table[WIDE_COUNT] * PLANES)
        & (global_y >= 0)
        & (global_y < table[NARROW_COUNT] * OWN)
    )
    background = jnp.where(mask > 0.5, m1, m0)
    out = []
    for threshold in thresholds:
        base = float(np.tanh(sharpness * threshold))
        scale = 1.0 / (base + float(np.tanh(sharpness * (1.0 - threshold))))
        projected = (base + jnp.tanh(sharpness * (density - threshold))) * scale
        permittivity = jnp.where(inside, m0 + projected * (m1 - m0), background)
        out.append(jnp.where(in_grid, time_step / permittivity, 0.0))
    return out


def first_message(ref, at):
    return [jnp.concatenate([ref[at + 4 * c + i] for i in range(4)], axis=0) for c in range(2)]


def first_state(r, block, table, ee_ref, h1_ref, far_ref, near_ref, step):
    core = table[CORE]
    far, near = first_message(far_ref, COARSE + r * FIRST_TILES), first_message(near_ref, r * FIRST_TILES)
    trace_h = [jnp.where(table[WIDE] == 0, 0.0, x) for x in select(core == 0, far, near)]
    trace_e = [jnp.where(table[WIDE] == table[WIDE_COUNT] - 1, 0.0, x) for x in select(core == 1, far, near)]
    e = {p: [ee_ref[block, c, p] for c in range(3)] for p in range(PLANES)}
    h = {p: [h1_ref[block, c, p] for c in range(3)] for p in range(PLANES)}
    top = PLANES - 1
    h[top] = [h[top][0], h[top][1] + step * trace_e[1], h[top][2] - step * trace_e[0]]
    below = jnp.where(table[WIDE] == 0, 0.0, step)
    h[-1] = [None, trace_h[0] + below * e[0][2], trace_h[1] - below * e[0][1]]
    return e, h


def as_message(traces):
    rows = lax.broadcasted_iota(jnp.int32, (8, LANES), 0)
    tiles = []
    for n in range(3):
        for c in range(2):
            tiles += tiles_of(traces[n][c], 3)
    halo = [[traces[n][c][OWN:] for c in range(2)] for n in range(3)]
    for c in range(2):
        tiles.append(jnp.where((rows > 1) & (rows < 5), pltpu.roll(halo[1][c], 4, 0), halo[0][c]))
    tiles.append(jnp.where(rows == 3, pltpu.roll(halo[2][1], 4, 0), halo[2][0]))
    return tiles


def from_message(tile):
    traces = []
    for n in range(3):
        step = []
        for c in range(2):
            halo = tile(20) if n == 2 else tile(18 + c)
            halo = pltpu.roll(halo, 4, 0) if n == 1 or (n == 2 and c == 1) else halo
            step.append(jnp.concatenate([tile((n * 2 + c) * 3 + i) for i in range(3)] + [halo], axis=0))
        traces.append(step)
    return traces


def refine(table, mine_ref, far_ref, wz_ref, wy_ref, d_ref):
    last = table[WIDE] == table[WIDE_COUNT] - 1
    coarse = [mine_ref[q] + far_ref[q] for q in range(COARSE)]
    coarse[5] = jnp.where(last, coarse[4], coarse[5])
    along_z = jnp.dot(
        jnp.concatenate(coarse, axis=0),
        wz_ref[...],
        precision=lax.Precision.HIGHEST,
        preferred_element_type=jnp.float32,
    )
    strips = [
        jnp.concatenate([along_z[8 * q : 8 * q + 8, :LANES], along_z[8 * q : 8 * q + 8, LANES:]], axis=0)
        for q in range(COARSE)
    ]
    along_y = jnp.dot(
        wy_ref[...],
        jnp.concatenate(strips, axis=1),
        precision=lax.Precision.HIGHEST,
        preferred_element_type=jnp.float32,
    )
    for q in range(COARSE):
        d_ref[q] = along_y[:, LANES * q : LANES * (q + 1)]


def plane_coefficients(p, mask, table, levels, d_ref, c_ref):
    q = 1 + p // 2
    density = d_ref[q] if p % 2 == 0 else 0.5 * (d_ref[q] + d_ref[q + 1])
    values = coefficients_of(density, mask, table[WIDE] * PLANES + p, table, levels, lane_ids())
    for r in range(3):
        c_ref[r, p + 1] = values[r]


def trace_kernel(
    table, levels, mine_ref, wz_ref, wy_ref, mm_ref, far_ref, near_ref, ee_ref, h1_ref, jj_ref,
    far_out, near_out, c_ref, d_ref,
):
    refine(table, mine_ref, far_ref, wz_ref, wy_ref, d_ref)
    for p in (0, 1, 2, 5, 6, 7):
        plane_coefficients(p, mm_ref[p], table, levels, d_ref, c_ref)
    lanes = lane_ids()
    step = step_of_rows(table[NARROW])
    core = table[CORE]
    zero = jnp.zeros((ROWS, LANES), jnp.float32)

    def per_real(r, carry):
        e, h = first_state(r, r, table, ee_ref, h1_ref, far_ref, near_ref, step)

        def electric(p):
            current = [jj_ref[c, p] for c in range(3)]
            e[p] = next_electric(e[p], h[p], (h[p - 1][1], h[p - 1][2]), c_ref[r, p + 1], current, lanes)

        def magnetic(p):
            h[p] = next_magnetic(h[p], e[p], (e[p + 1][1], e[p + 1][2]), step, lanes)

        for p in (0, 1, 2, 5, 6, 7):
            electric(p)
        h[-1] = [zero] * 3
        e[8] = [zero] * 3
        upward, downward = [], [(e[0][1], e[0][2])]
        for first in (5, 6, 7):
            for p in range(first, 8):
                magnetic(p)
            upward.append((h[7][1], h[7][2]))
            for p in range(first + 1, 8):
                electric(p)
        for last_plane in (1, 0):
            for p in range(last_plane + 1):
                magnetic(p)
            for p in range(last_plane + 1):
                electric(p)
            downward.append((e[0][1], e[0][2]))
        for i, (a, b) in enumerate(zip(as_message(upward), as_message(downward), strict=True)):
            far_out[r * TILES + i] = jnp.where(core == 1, a, b)
            near_out[r * TILES + i] = jnp.where(core == 1, b, a)
        return carry

    lax.fori_loop(0, 3, per_real, 0)


def stage_kernel(*refs):
    for source, copied in zip(refs[: len(refs) // 2], refs[len(refs) // 2 :], strict=True):
        copied[...] = source[...]


def inner_kernel(
    table, levels, mine_ref, wz_ref, wy_ref, mm_ref, far_ref, near_ref, ee_ref, h1_ref, jj_ref,
    eo_ref, ho_ref, c_ref, d_ref,
):
    r = pl.program_id(0)

    @pl.when(r == 0)
    def _():
        refine(table, mine_ref, far_ref, wz_ref, wy_ref, d_ref)
        core = table[CORE]
        far = jnp.concatenate([far_ref[COARSE + 3 * FIRST_TILES + i] for i in range(4)], axis=0)
        near = jnp.concatenate([near_ref[3 * FIRST_TILES + i] for i in range(4)], axis=0)
        for p in range(-1, PLANES + 1):
            if p < 0:
                mask = jnp.where(core == 0, far, near)
            else:
                mask = mm_ref[p] if p < PLANES else jnp.where(core == 1, far, near)
            plane_coefficients(p, mask, table, levels, d_ref, c_ref)

    lanes = lane_ids()
    step = step_of_rows(table[NARROW])
    e, h = first_state(r, 0, table, ee_ref, h1_ref, far_ref, near_ref, step)

    def electric(first, last):
        for p in range(first, last + 1):
            current = [jj_ref[c, p] for c in range(3)]
            e[p] = next_electric(e[p], h[p], (h[p - 1][1], h[p - 1][2]), c_ref[r, p + 1], current, lanes)

    def magnetic(first, last):
        for p in range(first, last + 1):
            h[p] = next_magnetic(h[p], e[p], (e[p + 1][1], e[p + 1][2]), step, lanes)

    electric(0, 7)
    magnetic(0, 6)
    electric(1, 6)
    magnetic(1, 5)
    electric(2, 5)
    magnetic(2, 4)
    electric(3, 4)
    for p in range(PLANES):
        for c in range(3):
            eo_ref[0, c, p] = e[p][c]
            ho_ref[0, c, p] = h[p][c]


def window_kernel(table, c_ref, far_ref, near_ref, ee_ref, hh_ref, jj_ref, eo_hbm, ho_hbm, eo_ref, ho_ref, sems):
    lanes = lane_ids()
    core = table[CORE]
    step = step_of_rows(table[NARROW])
    below = jnp.where(table[WIDE] == 0, 0.0, step)
    zero = jnp.zeros((ROWS, LANES), jnp.float32)

    def written(r):
        return [
            pltpu.make_async_copy(eo_ref.at[r], eo_hbm.at[r], sems.at[0, r]),
            pltpu.make_async_copy(ho_ref.at[r], ho_hbm.at[r], sems.at[1, r]),
        ]

    def per_real(r, carry):
        def tile_from_below(i):
            return jnp.where(core == 0, far_ref[r * TILES + i], near_ref[r * TILES + i])

        def tile_from_above(i):
            return jnp.where(core == 1, far_ref[r * TILES + i], near_ref[r * TILES + i])

        trace_h = from_message(tile_from_below)
        trace_e = from_message(tile_from_above)
        e = {p: [zero] * 3 for p in (-2, -1, 8, 9)}
        h = {p: [zero] * 3 for p in (-2, -1, 8)}
        for p in range(PLANES):
            e[p] = [ee_ref[r, c, p] for c in range(3)]
            h[p] = [hh_ref[r, c, p] for c in range(3)]

        def magnetic(planes, n):
            for p in planes:
                up = [e[p + 1][1], e[p + 1][2]]
                if p == 7:
                    up = [up[0] + trace_e[n - 2][0], up[1] + trace_e[n - 2][1]]
                h[p] = next_magnetic(h[p], e[p], up, below if p < 0 else step, lanes)

        def electric(planes, n):
            for p in planes:
                down = [h[p - 1][1], h[p - 1][2]]
                if p == 0:
                    down = [down[0] + trace_h[n - 2][0], down[1] + trace_h[n - 2][1]]
                current = [jj_ref[c, p] for c in range(3)] if 0 <= p < PLANES else None
                e[p] = next_electric(e[p], h[p], down, c_ref[r, p + 1], current, lanes)

        magnetic((-1, 7), 2)
        electric((0, 7, 8), 2)
        e[-1] = next_electric(e[-1], h[-1], (zero, zero), c_ref[r, 0], None, lanes)
        magnetic((-2, -1, 0, 6, 7, 8), 3)
        electric((-1, 0, 1, 6, 7, 8), 3)
        magnetic((-1, 0, 1, 5, 6, 7), 4)
        electric((0, 1, 2, 5, 6, 7), 4)
        for p in range(PLANES):
            for c in range(3):
                eo_ref[r, c, p] = e[p][c][:OWN]
                ho_ref[r, c, p] = h[p][c][:OWN]
        for copy in written(r):
            copy.start()
        return carry

    lax.fori_loop(0, 3, per_real, 0)
    for r in range(3):
        for copy in written(r):
            copy.wait()


def refine_weights():
    along_z = np.zeros((64, LANES), np.float32)
    for cell in range(LANES):
        along_z[cell // 2, cell] += 0.5
        along_z[min((cell + 1) // 2, 63), cell] += 0.5
    both = np.zeros((LANES, 2 * LANES), np.float32)
    both[:64, :LANES] = along_z
    both[64:, LANES:] = along_z
    along_y = np.zeros((ROWS, 16), np.float32)
    for row in range(ROWS):
        y = row if row < OWN + HALO else row - ROWS
        along_y[row, y // 2 + 2] += 0.5
        along_y[row, min((y + 1) // 2 + 2, 15)] += 0.5
    return both, along_y


def run(kernel, scalars, operands, outs, flops, scratch=(), steps=3, limit=60):
    def spec(shape, block):
        rank = len(shape)
        if block is pl.ANY:
            return pl.BlockSpec(memory_space=pl.ANY)
        if block is None:
            return pl.BlockSpec(tuple(shape), lambda r: (0,) * rank)
        if block is True:
            return pl.BlockSpec((1, *shape[1:]), lambda r: (r,) + (0,) * (rank - 1))
        block_shape, place = block
        return pl.BlockSpec(block_shape, lambda r: place)

    moved = sum(4 * int(np.prod(x.shape)) for x, _ in operands) + sum(4 * int(np.prod(x)) for x, _ in outs)
    return pl.pallas_call(
        kernel,
        grid=(steps,),
        in_specs=[pl.BlockSpec(memory_space=pltpu.SMEM)] * len(scalars)
        + [spec(x.shape, block) for x, block in operands],
        out_specs=[spec(shape, block) for shape, block in outs],
        out_shape=[jax.ShapeDtypeStruct(shape, jnp.float32) for shape, _ in outs],
        scratch_shapes=list(scratch),
        compiler_params=pltpu.CompilerParams(
            dimension_semantics=("arbitrary",), vmem_limit_bytes=limit * 1024 * 1024
        ),
        cost_estimate=pl.CostEstimate(flops=flops, bytes_accessed=moved, transcendentals=0),
        interpret=INTERPRET,
        name=kernel.__name__,
    )(*scalars, *[x for x, _ in operands])


def run_in_place(kernel, scalars, operands, outs, scratch, out_space, limit):
    return pl.pallas_call(
        kernel,
        in_specs=[pl.BlockSpec(memory_space=pltpu.SMEM)] * len(scalars)
        + [pl.BlockSpec(memory_space=pltpu.VMEM)] * len(operands),
        out_specs=[pl.BlockSpec(memory_space=out_space)] * len(outs),
        out_shape=[jax.ShapeDtypeStruct(shape, jnp.float32) for shape in outs],
        scratch_shapes=list(scratch),
        compiler_params=pltpu.CompilerParams(vmem_limit_bytes=limit * 1024 * 1024),
        cost_estimate=pl.CostEstimate(flops=10_000_000, bytes_accessed=10_000_000, transcendentals=0),
        interpret=INTERPRET,
        name=kernel.__name__,
    )(*scalars, *operands)


def body(
    electric,
    magnetic,
    current,
    density_tiles,
    tile_slabs,
    design_box,
    material_mask,
    material_levels,
):
    wide_count = lax.axis_size("wide")
    wide_place = lax.axis_index("wide")
    narrow_count = lax.axis_size("narrow")
    narrow_place = lax.axis_index("narrow")
    core = wide_place % 2
    half = wide_count // 2

    near_pairs = [(w, w ^ 1) for w in range(wide_count)]
    partner = [(w + 1) % wide_count if w % 2 else (w - 1) % wide_count for w in range(wide_count)]
    far_ring = [(w, partner[w]) for w in range(wide_count)]
    far_pairs = [(w, partner[w]) for w in range(1, wide_count - 1)]
    up = [(n, n + 1) for n in range(narrow_count - 1)]
    down = [(n + 1, n) for n in range(narrow_count - 1)]
    groups = [[w for w in range(wide_count) if (w // 2) % 2 == side] for side in range(2)]

    mate = jnp.where(wide_place % 2 == 1, wide_place + 1, wide_place - 1 + wide_count) % wide_count
    slabs = jnp.stack([wide_place, mate])[:, None] + jnp.arange(-1, 2, dtype=jnp.int32)[None, :]
    slabs = jnp.clip(slabs, 0, wide_count - 1)
    ids = jnp.arange(wide_count, dtype=jnp.int32)
    at = jnp.sum(jnp.where(tile_slabs[None, None, :] == slabs[:, :, None], ids, 0), axis=2)
    here = ((at // 2) % 2 == (wide_place // 2) % 2).astype(jnp.int32)
    place = (at // 4) * 2 + at % 2
    table = jnp.concatenate(
        [
            jnp.stack([wide_place, narrow_place, core, jnp.int32(wide_count), jnp.int32(narrow_count)]),
            design_box,
            jnp.stack([place, here], axis=1).reshape(12),
        ]
    ).astype(jnp.int32)

    stack = [
        electric.reshape(72, OWN, LANES),
        magnetic.reshape(72, OWN, LANES),
        current.reshape(24, OWN, LANES),
        material_mask,
    ]
    ends = [(x, ((x.shape[0], 8, LANES), (0, row, 0))) for x in stack for row in (0, 2)]
    halo = (HALO_PLANES, HALO, LANES)
    tile = jnp.transpose(density_tiles, (1, 0, 2))
    first_rows, last_rows, tile_first, tile_last = run(
        pack_kernel,
        (),
        ends + [(tile, None)],
        [(halo, None), (halo, None), ((4, LANES), None), ((4, LANES), None)],
        1_000_000,
        steps=1,
    )
    tile_lo = lax.ppermute(tile_last, "narrow", up)
    tile_hi = lax.ppermute(tile_first, "narrow", down)
    tile_lo, first_rows, last_rows = lax.optimization_barrier((tile_lo, first_rows, last_rows))
    low = lax.ppermute(last_rows, "narrow", up)
    high = lax.ppermute(first_rows, "narrow", down)
    (spread,) = run(
        tile_kernel,
        (table,),
        [(tile, None), (tile_lo, None), (tile_hi, None)],
        [((half, 4, 8, LANES), None)],
        1_000_000,
        steps=1,
        limit=8,
    )
    gathered = lax.all_to_all(spread, "wide", 0, 0, axis_index_groups=groups, tiled=True)
    gathered = gathered.reshape(half * 4, 8, LANES)

    extended = (3, 3, PLANES, ROWS, LANES)
    planes = (PLANES, ROWS, LANES)
    message = (3 * FIRST_TILES + 4, 8, LANES)
    e_ext, h_one, j_ext, m_ext, far, near = run(
        extend_kernel,
        (table,),
        [(electric, True), (magnetic, True), (current, None), (material_mask, None), (low, None), (high, None)],
        [(extended, True), (extended, True), ((3, *planes), None), (planes, None), ((COARSE + message[0], 8, LANES), None), (message, None)],
        100_000_000_000,
    )
    near = lax.ppermute(near, "wide", near_pairs)

    coarse = (COARSE, 8, LANES)
    mine, theirs = run(
        select_kernel,
        (table,),
        [(gathered, None)],
        [(coarse, None), (coarse, None)],
        1_000_000,
        steps=1,
        limit=8,
    )
    far = lax.dynamic_update_slice(far, theirs, (0, 0, 0))
    far = lax.ppermute(far, "wide", far_ring)
    fields = [(e_ext, True), (h_one, True), (j_ext, None)]

    weights_z, weights_y = refine_weights()
    message = (3 * TILES, 8, LANES)
    coefficients = (3, PLANES + 2, ROWS, LANES)
    strips = pltpu.VMEM((COARSE, ROWS, LANES), jnp.float32)
    still = (e_ext, h_one, j_ext, m_ext, weights_z, weights_y)
    e_on, h_on, j_on, m_on, z_on, y_on = run(
        stage_kernel,
        (),
        [(x, i < 2 or None) for i, x in enumerate(still)],
        [(x.shape, i < 2 or None) for i, x in enumerate(still)],
        1_000_000_000,
        limit=10,
    )
    far_end, near_end = run_in_place(
        trace_kernel,
        (table, material_levels),
        (mine, z_on, y_on, m_on, far, near, e_on, h_on, j_on),
        [message, message],
        [pltpu.VMEM(coefficients, jnp.float32), strips],
        pltpu.VMEM,
        16,
    )
    inputs = [(x, None) for x in (mine, weights_z, weights_y, m_ext, far, near)] + fields
    near_end = lax.ppermute(near_end, "wide", near_pairs)
    far_end = lax.ppermute(far_end, "wide", far_pairs)

    e_in, h_in, coefficient = run(
        inner_kernel,
        (table, material_levels),
        inputs,
        [(extended, True), (extended, True), (coefficients, None)],
        10_000_000,
        [strips],
        limit=24,
    )
    own = (3, 3, PLANES, OWN, LANES)
    return tuple(
        run_in_place(
            window_kernel,
            (table,),
            (coefficient, far_end, near_end, e_in, h_in, j_ext),
            [own, own],
            [pltpu.VMEM(own, jnp.float32), pltpu.VMEM(own, jnp.float32), pltpu.SemaphoreType.DMA((2, 3))],
            pltpu.HBM,
            16,
        )
    )


def solution(mesh):
    return jax.shard_map(
        body,
        mesh=mesh,
        in_specs=(
            P(None, None, "wide", "narrow", None),
            P(None, None, "wide", "narrow", None),
            P(None, "wide", "narrow", None),
            P("wide", "narrow", None),
            P(),
            P(),
            P("wide", "narrow", None),
            P(),
        ),
        out_specs=(P(None, None, "wide", "narrow", None), P(None, None, "wide", "narrow", None)),
        check_vma=False,
    )
```

```python
import jax
import jax.numpy as jnp
import numpy as np
from jax import lax
from jax.experimental import pallas as pl
from jax.experimental.pallas import tpu as pltpu
from jax.sharding import PartitionSpec as P

STEPS = 4
PLANES = 8
OWN = 24
ROWS = 32
HALO = 4
LANES = 128
FIRST_TILES = 8
COARSE = 6
TILES = 21

sharpness = 8.0
thresholds = (0.7, 0.5, 0.3)
time_step = 0.5

INTERPRET = False


def lane_ids():
    return lax.broadcasted_iota(jnp.int32, (ROWS, LANES), 1)


def row_ids():
    rows = lax.broadcasted_iota(jnp.int32, (ROWS, LANES), 0)
    return jnp.where(rows < OWN + HALO, rows, rows - ROWS)


def y_forward(a):
    return pltpu.roll(a, ROWS - 1, 0) - a


def y_backward(a):
    return a - pltpu.roll(a, 1, 0)


def z_forward(a, lanes):
    return jnp.where(lanes == LANES - 1, 0.0, pltpu.roll(a, LANES - 1, 1)) - a


def z_backward(a, lanes):
    return a - jnp.where(lanes == 0, 0.0, pltpu.roll(a, 1, 1))


def next_magnetic(h, e, e_up, step, lanes):
    up_y, up_z = e_up
    curl_x = y_forward(e[2]) - z_forward(e[1], lanes)
    curl_y = z_forward(e[0], lanes) - (up_z - e[2])
    curl_z = (up_y - e[1]) - y_forward(e[0])
    return [h[0] - step * curl_x, h[1] - step * curl_y, h[2] - step * curl_z]


def next_electric(e, h, h_down, coefficient, current, lanes):
    down_y, down_z = h_down
    curls = [
        y_backward(h[2]) - z_backward(h[1], lanes),
        z_backward(h[0], lanes) - (h[2] - down_z),
        (h[1] - down_y) - y_backward(h[0]),
    ]
    if current is not None:
        curls = [curls[c] - current[c] for c in range(3)]
    return [e[c] + coefficient * curls[c] for c in range(3)]


def step_of_rows(narrow_place):
    return jnp.where((row_ids() < 0) & (narrow_place == 0), 0.0, time_step)


WIDE, NARROW, CORE, WIDE_COUNT, NARROW_COUNT, BOX, MINE, THEIRS = 0, 1, 2, 3, 4, 5, 11, 17
E_AT, H_AT, J_AT, MASK_AT, HALO_PLANES = 0, 72, 144, 168, 176


def tiles_of(plane, count=4):
    return [plane[8 * i : 8 * i + 8] for i in range(count)]


def select(condition, yes, no):
    return [jnp.where(condition, a, b) for a, b in zip(yes, no, strict=True)]


def pack_kernel(
    e_first, e_last, h_first, h_last, j_first, j_last, m_first, m_last, tile_ref,
    first_ref, last_ref, tile_first, tile_last,
):
    tile_first[...] = jnp.concatenate([tile_ref[0], tile_ref[1]], axis=1)
    tile_last[...] = jnp.concatenate([tile_ref[10], tile_ref[11]], axis=1)
    for at, count, first, last in (
        (E_AT, 72, e_first, e_last),
        (H_AT, 72, h_first, h_last),
        (J_AT, 24, j_first, j_last),
        (MASK_AT, PLANES, m_first, m_last),
    ):
        first_ref[at : at + count] = first[:, :HALO].astype(jnp.float32)
        last_ref[at : at + count] = last[:, 8 - HALO :].astype(jnp.float32)


def tile_kernel(table, tile_ref, lo_ref, hi_ref, spread_ref):
    top = table[NARROW] == table[NARROW_COUNT] - 1
    for q in range(4):
        tile = jnp.concatenate([tile_ref[row, q : q + 1] for row in range(12)], axis=0)
        lo, hi = lo_ref[q : q + 1], hi_ref[q : q + 1]
        above = jnp.concatenate([hi[:, :64], hi[:, 64:]], axis=0)
        above = jnp.where(top, jnp.broadcast_to(tile[11:12], (2, 64)), above)
        first = jnp.concatenate([lo[:, :64], lo[:, 64:], tile[:6]], axis=0)
        second = jnp.concatenate([tile[6:], above], axis=0)
        packed = jnp.concatenate([first, second], axis=1)
        for i in range(spread_ref.shape[0]):
            spread_ref[i, q] = packed


def select_kernel(table, g_ref, mine_ref, theirs_ref):
    for at, ref in ((MINE, mine_ref), (THEIRS, theirs_ref)):
        for i, (which, q) in enumerate(((0, 3), (1, 0), (1, 1), (1, 2), (1, 3), (2, 0))):
            held = g_ref[table[at + which] * 4 + q]
            ref[i] = jnp.where(table[at + 3 + which] == 1, held, 0.0)


def extend_kernel(
    table, e_ref, h_ref, j_ref, m_ref, lo_ref, hi_ref, ee_ref, h1_ref, jj_ref, mm_ref, far_ref, near_ref
):
    r = pl.program_id(0)
    lanes = lane_ids()
    step = step_of_rows(table[NARROW])
    core = table[CORE]
    zero = jnp.zeros((ROWS, LANES), jnp.float32)

    def extended(own, at):
        return jnp.concatenate([own, hi_ref[at], lo_ref[at]], axis=0)

    up = [zero] * 3
    upward = downward = None
    for p in range(PLANES - 1, -1, -1):
        at = r * 24 + p
        e = [extended(e_ref[0, c, p], E_AT + at + c * PLANES) for c in range(3)]
        h = [extended(h_ref[0, c, p], H_AT + at + c * PLANES) for c in range(3)]
        new = next_magnetic(h, e, (up[1], up[2]), step, lanes)
        for c in range(3):
            ee_ref[0, c, p] = e[c]
            h1_ref[0, c, p] = new[c]
        if p == PLANES - 1:
            upward = tiles_of(new[1]) + tiles_of(new[2])
        if p == 0:
            downward = tiles_of(e[1]) + tiles_of(e[2])
        up = e
    far, near = select(core == 1, upward, downward), select(core == 1, downward, upward)
    for i in range(FIRST_TILES):
        far_ref[COARSE + r * FIRST_TILES + i] = far[i]
        near_ref[r * FIRST_TILES + i] = near[i]

    @pl.when(r == 0)
    def _():
        for p in range(PLANES):
            for c in range(3):
                jj_ref[c, p] = extended(j_ref[c, p], J_AT + c * PLANES + p)
            mm_ref[p] = extended(m_ref[p].astype(jnp.float32), MASK_AT + p)
        above, below = tiles_of(mm_ref[PLANES - 1]), tiles_of(mm_ref[0])
        far, near = select(core == 1, above, below), select(core == 1, below, above)
        for i in range(4):
            far_ref[COARSE + 3 * FIRST_TILES + i] = far[i]
            near_ref[3 * FIRST_TILES + i] = near[i]


def coefficients_of(density, mask, global_x, table, levels, lanes):
    m0, m1 = levels[0], levels[1]
    global_y = table[NARROW] * OWN + row_ids()
    inside = (
        (global_x >= table[BOX])
        & (global_x < table[BOX + 1])
        & (global_y >= table[BOX + 2])
        & (global_y < table[BOX + 3])
        & (lanes >= table[BOX + 4])
        & (lanes < table[BOX + 5])
    )
    in_grid = (
        (global_x >= 0)
        & (global_x < table[WIDE_COUNT] * PLANES)
        & (global_y >= 0)
        & (global_y < table[NARROW_COUNT] * OWN)
    )
    background = jnp.where(mask > 0.5, m1, m0)
    out = []
    for threshold in thresholds:
        base = float(np.tanh(sharpness * threshold))
        scale = 1.0 / (base + float(np.tanh(sharpness * (1.0 - threshold))))
        projected = (base + jnp.tanh(sharpness * (density - threshold))) * scale
        permittivity = jnp.where(inside, m0 + projected * (m1 - m0), background)
        out.append(jnp.where(in_grid, time_step / permittivity, 0.0))
    return out


def first_message(ref, at):
    return [jnp.concatenate([ref[at + 4 * c + i] for i in range(4)], axis=0) for c in range(2)]


def first_state(r, block, table, ee_ref, h1_ref, far_ref, near_ref, step):
    core = table[CORE]
    far, near = first_message(far_ref, COARSE + r * FIRST_TILES), first_message(near_ref, r * FIRST_TILES)
    trace_h = [jnp.where(table[WIDE] == 0, 0.0, x) for x in select(core == 0, far, near)]
    trace_e = [jnp.where(table[WIDE] == table[WIDE_COUNT] - 1, 0.0, x) for x in select(core == 1, far, near)]
    e = {p: [ee_ref[block, c, p] for c in range(3)] for p in range(PLANES)}
    h = {p: [h1_ref[block, c, p] for c in range(3)] for p in range(PLANES)}
    top = PLANES - 1
    h[top] = [h[top][0], h[top][1] + step * trace_e[1], h[top][2] - step * trace_e[0]]
    below = jnp.where(table[WIDE] == 0, 0.0, step)
    h[-1] = [None, trace_h[0] + below * e[0][2], trace_h[1] - below * e[0][1]]
    return e, h


def as_message(traces):
    rows = lax.broadcasted_iota(jnp.int32, (8, LANES), 0)
    tiles = []
    for n in range(3):
        for c in range(2):
            tiles += tiles_of(traces[n][c], 3)
    halo = [[traces[n][c][OWN:] for c in range(2)] for n in range(3)]
    for c in range(2):
        tiles.append(jnp.where((rows > 1) & (rows < 5), pltpu.roll(halo[1][c], 4, 0), halo[0][c]))
    tiles.append(jnp.where(rows == 3, pltpu.roll(halo[2][1], 4, 0), halo[2][0]))
    return tiles


def from_message(tile):
    traces = []
    for n in range(3):
        step = []
        for c in range(2):
            halo = tile(20) if n == 2 else tile(18 + c)
            halo = pltpu.roll(halo, 4, 0) if n == 1 or (n == 2 and c == 1) else halo
            step.append(jnp.concatenate([tile((n * 2 + c) * 3 + i) for i in range(3)] + [halo], axis=0))
        traces.append(step)
    return traces


def refine(table, mine_ref, far_ref, wz_ref, wy_ref, d_ref):
    last = table[WIDE] == table[WIDE_COUNT] - 1
    coarse = [mine_ref[q] + far_ref[q] for q in range(COARSE)]
    coarse[5] = jnp.where(last, coarse[4], coarse[5])
    along_z = jnp.dot(
        jnp.concatenate(coarse, axis=0),
        wz_ref[...],
        precision=lax.Precision.HIGHEST,
        preferred_element_type=jnp.float32,
    )
    strips = [
        jnp.concatenate([along_z[8 * q : 8 * q + 8, :LANES], along_z[8 * q : 8 * q + 8, LANES:]], axis=0)
        for q in range(COARSE)
    ]
    along_y = jnp.dot(
        wy_ref[...],
        jnp.concatenate(strips, axis=1),
        precision=lax.Precision.HIGHEST,
        preferred_element_type=jnp.float32,
    )
    for q in range(COARSE):
        d_ref[q] = along_y[:, LANES * q : LANES * (q + 1)]


def plane_coefficients(p, mask, table, levels, d_ref, c_ref):
    q = 1 + p // 2
    density = d_ref[q] if p % 2 == 0 else 0.5 * (d_ref[q] + d_ref[q + 1])
    values = coefficients_of(density, mask, table[WIDE] * PLANES + p, table, levels, lane_ids())
    for r in range(3):
        c_ref[r, p + 1] = values[r]


def trace_kernel(
    table, levels, mine_ref, wz_ref, wy_ref, mm_ref, far_ref, near_ref, ee_ref, h1_ref, jj_ref,
    far_out, near_out, c_ref, d_ref,
):
    refine(table, mine_ref, far_ref, wz_ref, wy_ref, d_ref)
    for p in (0, 1, 2, 5, 6, 7):
        plane_coefficients(p, mm_ref[p], table, levels, d_ref, c_ref)
    lanes = lane_ids()
    step = step_of_rows(table[NARROW])
    core = table[CORE]
    zero = jnp.zeros((ROWS, LANES), jnp.float32)

    def per_real(r, carry):
        e, h = first_state(r, r, table, ee_ref, h1_ref, far_ref, near_ref, step)

        def electric(p):
            current = [jj_ref[c, p] for c in range(3)]
            e[p] = next_electric(e[p], h[p], (h[p - 1][1], h[p - 1][2]), c_ref[r, p + 1], current, lanes)

        def magnetic(p):
            h[p] = next_magnetic(h[p], e[p], (e[p + 1][1], e[p + 1][2]), step, lanes)

        for p in (0, 1, 2, 5, 6, 7):
            electric(p)
        h[-1] = [zero] * 3
        e[8] = [zero] * 3
        upward, downward = [], [(e[0][1], e[0][2])]
        for first in (5, 6, 7):
            for p in range(first, 8):
                magnetic(p)
            upward.append((h[7][1], h[7][2]))
            for p in range(first + 1, 8):
                electric(p)
        for last_plane in (1, 0):
            for p in range(last_plane + 1):
                magnetic(p)
            for p in range(last_plane + 1):
                electric(p)
            downward.append((e[0][1], e[0][2]))
        for i, (a, b) in enumerate(zip(as_message(upward), as_message(downward), strict=True)):
            far_out[r * TILES + i] = jnp.where(core == 1, a, b)
            near_out[r * TILES + i] = jnp.where(core == 1, b, a)
        return carry

    lax.fori_loop(0, 3, per_real, 0)


def stage_kernel(*refs):
    for source, copied in zip(refs[: len(refs) // 2], refs[len(refs) // 2 :], strict=True):
        copied[...] = source[...]


def inner_kernel(
    table, levels, mine_ref, wz_ref, wy_ref, mm_ref, far_ref, near_ref, ee_ref, h1_ref, jj_ref,
    eo_ref, ho_ref, c_ref, d_ref,
):
    r = pl.program_id(0)

    @pl.when(r == 0)
    def _():
        refine(table, mine_ref, far_ref, wz_ref, wy_ref, d_ref)
        core = table[CORE]
        far = jnp.concatenate([far_ref[COARSE + 3 * FIRST_TILES + i] for i in range(4)], axis=0)
        near = jnp.concatenate([near_ref[3 * FIRST_TILES + i] for i in range(4)], axis=0)
        for p in range(-1, PLANES + 1):
            if p < 0:
                mask = jnp.where(core == 0, far, near)
            else:
                mask = mm_ref[p] if p < PLANES else jnp.where(core == 1, far, near)
            plane_coefficients(p, mask, table, levels, d_ref, c_ref)

    lanes = lane_ids()
    step = step_of_rows(table[NARROW])
    e, h = first_state(r, 0, table, ee_ref, h1_ref, far_ref, near_ref, step)

    def electric(first, last):
        for p in range(first, last + 1):
            current = [jj_ref[c, p] for c in range(3)]
            e[p] = next_electric(e[p], h[p], (h[p - 1][1], h[p - 1][2]), c_ref[r, p + 1], current, lanes)

    def magnetic(first, last):
        for p in range(first, last + 1):
            h[p] = next_magnetic(h[p], e[p], (e[p + 1][1], e[p + 1][2]), step, lanes)

    electric(0, 7)
    magnetic(0, 6)
    electric(1, 6)
    magnetic(1, 5)
    electric(2, 5)
    magnetic(2, 4)
    electric(3, 4)
    for p in range(PLANES):
        for c in range(3):
            eo_ref[0, c, p] = e[p][c]
            ho_ref[0, c, p] = h[p][c]


def window_kernel(table, c_ref, far_ref, near_ref, ee_ref, hh_ref, jj_ref, eo_hbm, ho_hbm, eo_ref, ho_ref, sems):
    lanes = lane_ids()
    core = table[CORE]
    step = step_of_rows(table[NARROW])
    below = jnp.where(table[WIDE] == 0, 0.0, step)
    zero = jnp.zeros((ROWS, LANES), jnp.float32)

    def written(r):
        return [
            pltpu.make_async_copy(eo_ref.at[r], eo_hbm.at[r], sems.at[0, r]),
            pltpu.make_async_copy(ho_ref.at[r], ho_hbm.at[r], sems.at[1, r]),
        ]

    def per_real(r, carry):
        def tile_from_below(i):
            return jnp.where(core == 0, far_ref[r * TILES + i], near_ref[r * TILES + i])

        def tile_from_above(i):
            return jnp.where(core == 1, far_ref[r * TILES + i], near_ref[r * TILES + i])

        trace_h = from_message(tile_from_below)
        trace_e = from_message(tile_from_above)
        e = {p: [zero] * 3 for p in (-2, -1, 8, 9)}
        h = {p: [zero] * 3 for p in (-2, -1, 8)}
        for p in range(PLANES):
            e[p] = [ee_ref[r, c, p] for c in range(3)]
            h[p] = [hh_ref[r, c, p] for c in range(3)]

        def magnetic(planes, n):
            for p in planes:
                up = [e[p + 1][1], e[p + 1][2]]
                if p == 7:
                    up = [up[0] + trace_e[n - 2][0], up[1] + trace_e[n - 2][1]]
                h[p] = next_magnetic(h[p], e[p], up, below if p < 0 else step, lanes)

        def electric(planes, n):
            for p in planes:
                down = [h[p - 1][1], h[p - 1][2]]
                if p == 0:
                    down = [down[0] + trace_h[n - 2][0], down[1] + trace_h[n - 2][1]]
                current = [jj_ref[c, p] for c in range(3)] if 0 <= p < PLANES else None
                e[p] = next_electric(e[p], h[p], down, c_ref[r, p + 1], current, lanes)

        magnetic((-1, 7), 2)
        electric((0, 7, 8), 2)
        e[-1] = next_electric(e[-1], h[-1], (zero, zero), c_ref[r, 0], None, lanes)
        magnetic((-2, -1, 0, 6, 7, 8), 3)
        electric((-1, 0, 1, 6, 7, 8), 3)
        magnetic((-1, 0, 1, 5, 6, 7), 4)
        electric((0, 1, 2, 5, 6, 7), 4)
        for p in range(PLANES):
            for c in range(3):
                eo_ref[r, c, p] = e[p][c][:OWN]
                ho_ref[r, c, p] = h[p][c][:OWN]
        for copy in written(r):
            copy.start()
        return carry

    lax.fori_loop(0, 3, per_real, 0)
    for r in range(3):
        for copy in written(r):
            copy.wait()


def refine_weights():
    along_z = np.zeros((64, LANES), np.float32)
    for cell in range(LANES):
        along_z[cell // 2, cell] += 0.5
        along_z[min((cell + 1) // 2, 63), cell] += 0.5
    both = np.zeros((LANES, 2 * LANES), np.float32)
    both[:64, :LANES] = along_z
    both[64:, LANES:] = along_z
    along_y = np.zeros((ROWS, 16), np.float32)
    for row in range(ROWS):
        y = row if row < OWN + HALO else row - ROWS
        along_y[row, y // 2 + 2] += 0.5
        along_y[row, min((y + 1) // 2 + 2, 15)] += 0.5
    return both, along_y


def run(kernel, scalars, operands, outs, flops, scratch=(), steps=3, limit=60):
    def spec(shape, block):
        rank = len(shape)
        if block is pl.ANY:
            return pl.BlockSpec(memory_space=pl.ANY)
        if block == 'halves':
            return pl.BlockSpec((shape[0] // 2, *shape[1:]), lambda r: (r,) + (0,) * (rank - 1))
        if block is None:
            return pl.BlockSpec(tuple(shape), lambda r: (0,) * rank)
        if block is True:
            return pl.BlockSpec((1, *shape[1:]), lambda r: (r,) + (0,) * (rank - 1))
        block_shape, place = block
        return pl.BlockSpec(block_shape, lambda r: place)

    moved = sum(4 * int(np.prod(x.shape)) for x, _ in operands) + sum(4 * int(np.prod(x)) for x, _ in outs)
    return pl.pallas_call(
        kernel,
        grid=(steps,),
        in_specs=[pl.BlockSpec(memory_space=pltpu.SMEM)] * len(scalars)
        + [spec(x.shape, block) for x, block in operands],
        out_specs=[spec(shape, block) for shape, block in outs],
        out_shape=[jax.ShapeDtypeStruct(shape, jnp.float32) for shape, _ in outs],
        scratch_shapes=list(scratch),
        compiler_params=pltpu.CompilerParams(
            dimension_semantics=("arbitrary",), vmem_limit_bytes=limit * 1024 * 1024
        ),
        cost_estimate=pl.CostEstimate(flops=flops, bytes_accessed=moved, transcendentals=0),
        interpret=INTERPRET,
        name=kernel.__name__,
    )(*scalars, *[x for x, _ in operands])


def run_in_place(kernel, scalars, operands, outs, scratch, out_space, limit):
    return pl.pallas_call(
        kernel,
        in_specs=[pl.BlockSpec(memory_space=pltpu.SMEM)] * len(scalars)
        + [pl.BlockSpec(memory_space=pltpu.VMEM)] * len(operands),
        out_specs=[pl.BlockSpec(memory_space=out_space)] * len(outs),
        out_shape=[jax.ShapeDtypeStruct(shape, jnp.float32) for shape in outs],
        scratch_shapes=list(scratch),
        compiler_params=pltpu.CompilerParams(vmem_limit_bytes=limit * 1024 * 1024),
        cost_estimate=pl.CostEstimate(flops=10_000_000, bytes_accessed=10_000_000, transcendentals=0),
        interpret=INTERPRET,
        name=kernel.__name__,
    )(*scalars, *operands)


def body(
    electric,
    magnetic,
    current,
    density_tiles,
    tile_slabs,
    design_box,
    material_mask,
    material_levels,
):
    wide_count = lax.axis_size("wide")
    wide_place = lax.axis_index("wide")
    narrow_count = lax.axis_size("narrow")
    narrow_place = lax.axis_index("narrow")
    core = wide_place % 2
    half = wide_count // 2

    near_pairs = [(w, w ^ 1) for w in range(wide_count)]
    partner = [(w + 1) % wide_count if w % 2 else (w - 1) % wide_count for w in range(wide_count)]
    far_ring = [(w, partner[w]) for w in range(wide_count)]
    far_pairs = [(w, partner[w]) for w in range(1, wide_count - 1)]
    up = [(n, n + 1) for n in range(narrow_count - 1)]
    down = [(n + 1, n) for n in range(narrow_count - 1)]
    groups = [[w for w in range(wide_count) if (w // 2) % 2 == side] for side in range(2)]

    mate = jnp.where(wide_place % 2 == 1, wide_place + 1, wide_place - 1 + wide_count) % wide_count
    slabs = jnp.stack([wide_place, mate])[:, None] + jnp.arange(-1, 2, dtype=jnp.int32)[None, :]
    slabs = jnp.clip(slabs, 0, wide_count - 1)
    ids = jnp.arange(wide_count, dtype=jnp.int32)
    at = jnp.sum(jnp.where(tile_slabs[None, None, :] == slabs[:, :, None], ids, 0), axis=2)
    here = ((at // 2) % 2 == (wide_place // 2) % 2).astype(jnp.int32)
    place = (at // 4) * 2 + at % 2
    table = jnp.concatenate(
        [
            jnp.stack([wide_place, narrow_place, core, jnp.int32(wide_count), jnp.int32(narrow_count)]),
            design_box,
            jnp.stack([place, here], axis=1).reshape(12),
        ]
    ).astype(jnp.int32)

    stack = [
        electric.reshape(72, OWN, LANES),
        magnetic.reshape(72, OWN, LANES),
        current.reshape(24, OWN, LANES),
        material_mask,
    ]
    ends = [(x, ((x.shape[0], 8, LANES), (0, row, 0))) for x in stack for row in (0, 2)]
    halo = (HALO_PLANES, HALO, LANES)
    tile = jnp.transpose(density_tiles, (1, 0, 2))
    first_rows, last_rows, tile_first, tile_last = run(
        pack_kernel,
        (),
        ends + [(tile, None)],
        [(halo, None), (halo, None), ((4, LANES), None), ((4, LANES), None)],
        1_000_000,
        steps=1,
    )
    tile_lo = lax.ppermute(tile_last, "narrow", up)
    tile_hi = lax.ppermute(tile_first, "narrow", down)
    tile_lo, first_rows, last_rows = lax.optimization_barrier((tile_lo, first_rows, last_rows))
    low = lax.ppermute(last_rows, "narrow", up)
    high = lax.ppermute(first_rows, "narrow", down)
    (spread,) = run(
        tile_kernel,
        (table,),
        [(tile, None), (tile_lo, None), (tile_hi, None)],
        [((half, 4, 8, LANES), 'halves')],
        1_000_000,
        steps=2,
        limit=8,
    )
    gathered = lax.all_to_all(spread, "wide", 0, 0, axis_index_groups=groups, tiled=True)
    gathered = gathered.reshape(half * 4, 8, LANES)

    extended = (3, 3, PLANES, ROWS, LANES)
    planes = (PLANES, ROWS, LANES)
    message = (3 * FIRST_TILES + 4, 8, LANES)
    e_ext, h_one, j_ext, m_ext, far, near = run(
        extend_kernel,
        (table,),
        [(electric, True), (magnetic, True), (current, None), (material_mask, None), (low, None), (high, None)],
        [(extended, True), (extended, True), ((3, *planes), None), (planes, None), ((COARSE + message[0], 8, LANES), None), (message, None)],
        100_000_000_000,
    )
    near = lax.ppermute(near, "wide", near_pairs)

    coarse = (COARSE, 8, LANES)
    mine, theirs = run(
        select_kernel,
        (table,),
        [(gathered, None)],
        [(coarse, None), (coarse, None)],
        1_000_000,
        steps=1,
        limit=8,
    )
    far = lax.dynamic_update_slice(far, theirs, (0, 0, 0))
    far = lax.ppermute(far, "wide", far_ring)
    fields = [(e_ext, True), (h_one, True), (j_ext, None)]

    weights_z, weights_y = refine_weights()
    message = (3 * TILES, 8, LANES)
    coefficients = (3, PLANES + 2, ROWS, LANES)
    strips = pltpu.VMEM((COARSE, ROWS, LANES), jnp.float32)
    still = (e_ext, h_one, j_ext, m_ext, weights_z, weights_y)
    e_on, h_on, j_on, m_on, z_on, y_on = run(
        stage_kernel,
        (),
        [(x, i < 2 or None) for i, x in enumerate(still)],
        [(x.shape, i < 2 or None) for i, x in enumerate(still)],
        1_000_000_000,
        limit=10,
    )
    far_end, near_end = run_in_place(
        trace_kernel,
        (table, material_levels),
        (mine, z_on, y_on, m_on, far, near, e_on, h_on, j_on),
        [message, message],
        [pltpu.VMEM(coefficients, jnp.float32), strips],
        pltpu.VMEM,
        16,
    )
    inputs = [(x, None) for x in (mine, weights_z, weights_y, m_ext, far, near)] + fields
    near_end = lax.ppermute(near_end, "wide", near_pairs)
    far_end = lax.ppermute(far_end, "wide", far_pairs)

    e_in, h_in, coefficient = run(
        inner_kernel,
        (table, material_levels),
        inputs,
        [(extended, True), (extended, True), (coefficients, None)],
        10_000_000,
        [strips],
        limit=24,
    )
    own = (3, 3, PLANES, OWN, LANES)
    return tuple(
        run_in_place(
            window_kernel,
            (table,),
            (coefficient, far_end, near_end, e_in, h_in, j_ext),
            [own, own],
            [pltpu.VMEM(own, jnp.float32), pltpu.VMEM(own, jnp.float32), pltpu.SemaphoreType.DMA((2, 3))],
            pltpu.HBM,
            16,
        )
    )


def solution(mesh):
    return jax.shard_map(
        body,
        mesh=mesh,
        in_specs=(
            P(None, None, "wide", "narrow", None),
            P(None, None, "wide", "narrow", None),
            P(None, "wide", "narrow", None),
            P("wide", "narrow", None),
            P(),
            P(),
            P("wide", "narrow", None),
            P(),
        ),
        out_specs=(P(None, None, "wide", "narrow", None), P(None, None, "wide", "narrow", None)),
        check_vma=False,
    )
```
